128 devices in a mesh: cfg: 2 (over z_lo), req: 8 (over z_hi, x), seq: 8 (over y, core).
Axes of the slice: x: 4, y: 4, z: 4 (z_hi: 2, z_lo: 2; z = z_hi * 2 + z_lo), core: 2. Of those that a mesh axis runs over, the one named last changes fastest.
Arguments:
- img_state: bfloat16 [2, 16, 1024, 1536], P('cfg', 'req', 'seq'), may hold values from -6 to 6
- txt_state: bfloat16 [2, 16, 192, 1536], P('cfg', 'req', 'seq'), may hold values from -6 to 6
- cond_vec: float32 [2, 16, 1536], P('cfg'), may hold values from -6 to 6
- text_len: int32 [2, 16], P('cfg', 'req'), may hold values from 38 to 154, as said below
- latent: float32 [16, 1024, 64], P('req', 'seq', 'cfg'), may hold values from -6 to 6
- w_mod: bfloat16 [15360, 1536], P(('req', 'seq')), may hold values from -0.15625 to 0.15625
- w_qkv_img: bfloat16 [3, 1536, 1536], P(None, 'seq')
- w_qkv_txt: bfloat16 [3, 1536, 1536], P(None, 'seq')
- w_attn_out: bfloat16 [1536, 1536], P('seq'), may hold values from -2 to 2
- w_up: bfloat16 [6144, 1536], P(('cfg', 'req', 'seq')), may hold values from -0.15625 to 0.15625
- w_down: bfloat16 [6144, 1536], P(('cfg', 'req', 'seq')), may hold values from -0.078125 to 0.078125
- w_final: bfloat16 [1536, 64], replicated, may hold values from -0.078125 to 0.078125
Outputs:
- velocity: float32 [16, 1024, 64], P('req', 'seq', 'cfg')
- latent_next: float32 [16, 1024, 64], P('req', 'seq', 'cfg')
The draws below stay inside these ranges and needn't reach their ends.
Inputs may be any that keep to these rules, and one draw needn't show every extreme that they name: Text slot t of prompt p in branch c is live when t < text_len[c, p]; every draw has a length equal to 154.
All inputs are finite; a program needn't handle non-finite values.
Results may differ from the reference program's by a relative error of at most 0.02.
Values may be sent and summed in bfloat16 or wider, within the bound.
No kernel may reach another device: no remote copies, remote signals or barrier semaphores. Data moves between devices by JAX's collectives and lax.ppermute only.
A program may use at most 128 MiB of HBM per device.

```python
import jax
import jax.numpy as jnp
from jax import lax

D = 1536
FF = 6144
HEAD = 64
PCH = 64
IMG = 1024
TXT = 192
TXT_MAX = 154
HEADS = 24
PROMPTS = 16


def draw_text_len(key, part):
    lengths = jax.random.randint(key, (2 * PROMPTS,), TXT_MAX // 4, TXT_MAX + 1)
    place = jax.random.randint(jax.random.fold_in(key, 7), (), 0, 2 * PROMPTS)
    lengths = jnp.where(jnp.arange(2 * PROMPTS) == place, TXT_MAX, lengths)
    return lengths.reshape(2, PROMPTS).astype(jnp.int32)


def projection_draw(key):
    base = jax.random.normal(key, (3, D, D), jnp.float32) * D ** (-0.5)
    return base


def draw_w_qkv_img(key, part):
    return projection_draw(jax.random.fold_in(key, 11)).astype(jnp.bfloat16)


def draw_w_qkv_txt(key, part):
    return projection_draw(jax.random.fold_in(key, 12)).astype(jnp.bfloat16)


def steps_of(key, shape, shards, low, high):
    def one(axis_at, blocks):
        draws = jax.random.uniform(jax.random.fold_in(jax.random.fold_in(key, 6), axis_at), (blocks,), jnp.float32, low / len(shards), high / len(shards))
        return jnp.repeat(jnp.exp(draws), shape[axis_at] // blocks).reshape((-1,) + (1,) * (len(shape) - axis_at - 1))

    level = one(*shards[0])
    for cut in shards[1:]:
        level = level * one(*cut)
    return level


def bell_draw(stream_key, dims, deviation, limit, cuts=(), held_as=jnp.bfloat16):
    factor_of = steps_of(stream_key, dims, cuts, -0.22, 0.18) if cuts else 1.0
    array = jax.random.normal(stream_key, dims, jnp.float32) * deviation * factor_of
    return jnp.minimum(jnp.maximum(array, -limit), limit).astype(held_as)


def setup_inputs(seed: int = 0) -> dict:
    arg_keys = jax.random.split(jax.random.key(seed), 13)
    img_state = bell_draw(arg_keys[0], (2, PROMPTS, IMG, D), 1.0, 6.0, ((0, 2), (1, 8), (2, 8)))
    txt_state = bell_draw(arg_keys[1], (2, PROMPTS, TXT, D), 1.0, 6.0, ((0, 2), (1, 8), (2, 8)))
    cond_vec = bell_draw(arg_keys[2], (2, PROMPTS, D), 1.0, 6.0, ((0, 2),), jnp.float32)
    text_len = draw_text_len(jax.random.fold_in(arg_keys[12], 71), 0)
    latent = bell_draw(arg_keys[4], (PROMPTS, IMG, PCH), 1.0, 6.0, ((0, 8), (1, 8), (2, 2)), jnp.float32)
    w_mod = bell_draw(arg_keys[5], (10 * D, D), D ** -0.5, 0.15625, ((0, 64),))
    w_qkv_img = draw_w_qkv_img(jax.random.fold_in(arg_keys[12], 71), 0)
    w_qkv_txt = draw_w_qkv_txt(jax.random.fold_in(arg_keys[12], 71), 0)
    w_attn_out = bell_draw(arg_keys[8], (D, D), 0.15, 2.0, ((0, 8),))
    w_up = bell_draw(arg_keys[9], (FF, D), D ** -0.5, 0.15625, ((0, 128),))
    w_down = bell_draw(arg_keys[10], (FF, D), FF ** -0.5, 0.078125, ((0, 128),))
    w_final = bell_draw(arg_keys[11], (D, PCH), 0.005, 0.078125)
    return {"img_state": img_state, "txt_state": txt_state, "cond_vec": cond_vec, "text_len": text_len, "latent": latent, "w_mod": w_mod, "w_qkv_img": w_qkv_img, "w_qkv_txt": w_qkv_txt, "w_attn_out": w_attn_out, "w_up": w_up, "w_down": w_down, "w_final": w_final}


def layer_norm(value):
    mean = lax.optimization_barrier(jnp.mean(value, axis=-1, keepdims=True))
    centered = value - mean
    spread = lax.optimization_barrier(jnp.mean(centered * centered, axis=-1, keepdims=True))
    return centered * lax.rsqrt(spread + 1e-06)

def one_stream(img, txt, mod, length, w_qkv_img, w_qkv_txt, w_attn_out, w_up, w_down, w_final):
    parts = mod.reshape(10, D)
    a_img = (layer_norm(img.astype(jnp.float32)) * (1.0 + parts[1]) + parts[0]).astype(jnp.bfloat16)
    a_txt = (layer_norm(txt.astype(jnp.float32)) * (1.0 + parts[7]) + parts[6]).astype(jnp.bfloat16)
    qkv_img = jnp.einsum('nd,jed->jne', a_img.astype(jnp.float32), w_qkv_img.astype(jnp.float32)).astype(jnp.bfloat16)
    qkv_txt = jnp.einsum('nd,jed->jne', a_txt.astype(jnp.float32), w_qkv_txt.astype(jnp.float32)).astype(jnp.bfloat16)
    query = qkv_img[0].reshape(IMG, HEADS, HEAD).astype(jnp.float32)
    keys = jnp.concatenate([qkv_img[1], qkv_txt[1]], axis=0).reshape(IMG + TXT, HEADS, HEAD).astype(jnp.float32)
    values = jnp.concatenate([qkv_img[2], qkv_txt[2]], axis=0).reshape(IMG + TXT, HEADS, HEAD).astype(jnp.float32)
    scores = jnp.einsum('qhe,khe->hqk', query, keys) * HEAD ** (-0.5)
    slots = jnp.arange(IMG + TXT)
    live = slots < IMG + length
    scores = jnp.where(live[None, None, :], scores, -1e+30)
    probs = jax.nn.softmax(scores, axis=-1).astype(jnp.bfloat16)
    attended = jnp.einsum('hqk,khe->qhe', probs.astype(jnp.float32), values).astype(jnp.bfloat16).reshape(IMG, D)
    proj = jnp.dot(attended, w_attn_out, preferred_element_type=jnp.float32)
    resid_one = (img.astype(jnp.float32) + parts[2] * proj).astype(jnp.bfloat16)
    normed = (layer_norm(resid_one.astype(jnp.float32)) * (1.0 + parts[4]) + parts[3]).astype(jnp.bfloat16)
    inner = lax.dot_general(normed, w_up, (((1,), (1,)), ((), ())), preferred_element_type=jnp.float32)
    hidden = jax.nn.gelu(inner, approximate=True).astype(jnp.bfloat16)
    mlp_out = jnp.dot(hidden, w_down, preferred_element_type=jnp.float32)
    resid_two = resid_one.astype(jnp.float32) + parts[5] * mlp_out
    final_in = (layer_norm(resid_two) * (1.0 + parts[9]) + parts[8]).astype(jnp.bfloat16)
    return jnp.dot(final_in, w_final, preferred_element_type=jnp.float32)

def reference(img_state, txt_state, cond_vec, text_len, latent, w_mod, w_qkv_img, w_qkv_txt, w_attn_out, w_up, w_down, w_final):
    cond_act = jax.nn.silu(cond_vec).astype(jnp.bfloat16)
    mod = jnp.einsum('cpd,ed->cpe', cond_act.astype(jnp.float32), w_mod.astype(jnp.float32))

    def run_item(item):
        return one_stream(item[0], item[1], item[2], item[3], w_qkv_img, w_qkv_txt, w_attn_out, w_up, w_down, w_final)
    items = (img_state.reshape(2 * PROMPTS, IMG, D), txt_state.reshape(2 * PROMPTS, TXT, D), mod.reshape(2 * PROMPTS, 10 * D), text_len.reshape(2 * PROMPTS))
    branch_vel = lax.map(run_item, items).reshape(2, PROMPTS, IMG, PCH)
    velocity = branch_vel[1] + 4.5 * (branch_vel[0] - branch_vel[1])
    latent_next = latent - 0.04 * velocity
    return (velocity, latent_next)
```

```python
import math

import jax
import jax.numpy as jnp
import numpy as np
from jax import lax
from jax.experimental import pallas as pl
from jax.experimental.pallas import tpu as pltpu
from jax.sharding import Mesh
from jax.sharding import PartitionSpec as P

HEAD = 64
SEQ = ("y", "core")
REQ = ("zhi", "x")
NT = (((1,), (1,)), ((), ()))
NN = (((1,), (0,)), ((), ()))
TXT_PAD = 32


def dot(a, b, dims):
    return lax.dot_general(a, b, dims, preferred_element_type=jnp.float32)


def layer_norm(value):
    mean = jnp.mean(value, axis=-1, keepdims=True)
    centered = value - mean
    spread = jnp.mean(centered * centered, axis=-1, keepdims=True)
    return centered * lax.rsqrt(spread + 1e-06)


def attn_kernel(seqs, rows, txt, x_ref, mod_ref, bias_ref, wi_ref, wt_ref, out_ref, ai, at, k_s, v_s, q_s):
    block = rows + TXT_PAD
    img = seqs * rows
    keys = seqs * block
    for s in range(seqs):
        part = x_ref[0, s * block : s * block + rows, :].astype(jnp.float32)
        normed = layer_norm(part) * (1.0 + mod_ref[0, 1:2, :]) + mod_ref[0, 0:1, :]
        ai[s * rows : (s + 1) * rows, :] = normed.astype(jnp.bfloat16)
        part = x_ref[0, s * block + rows : (s + 1) * block, :].astype(jnp.float32)
        normed = layer_norm(part) * (1.0 + mod_ref[0, 7:8, :]) + mod_ref[0, 6:7, :]
        at[s * TXT_PAD : (s + 1) * TXT_PAD, :] = normed.astype(jnp.bfloat16)
    width = wi_ref.shape[1]
    heads = width // HEAD
    a_img, a_txt = ai[...], at[...]
    k_s[0:img, :] = dot(a_img, wi_ref[1], NT).astype(jnp.bfloat16)
    k_s[img:keys, :] = dot(a_txt, wt_ref[1], NT).astype(jnp.bfloat16)
    q_s[...] = (dot(wi_ref[0], a_img, NT) * (HEAD ** (-0.5) * math.log2(math.e))).astype(jnp.bfloat16)
    v_img = dot(wi_ref[2], a_img, NT).astype(jnp.bfloat16)
    v_txt = dot(wt_ref[2], a_txt, NT).astype(jnp.bfloat16)
    ones = jnp.ones((16, keys), jnp.bfloat16)
    for h in range(heads):
        v_s[h, 0:HEAD, 0:img] = v_img[h * HEAD : (h + 1) * HEAD, :]
        v_s[h, 0:HEAD, img:keys] = v_txt[h * HEAD : (h + 1) * HEAD, :]
        v_s[h, HEAD : HEAD + 16, :] = ones
    step = 256
    k_all = k_s[...]
    bias = bias_ref[0]
    for h in range(heads):
        for c in range(img // step):
            q_h = q_s[h * HEAD : (h + 1) * HEAD, c * step : (c + 1) * step]
            pieces = []
            if h:
                pieces.append(jnp.zeros((h * HEAD, step), jnp.bfloat16))
            pieces.append(q_h)
            if h + 1 < heads:
                pieces.append(jnp.zeros(((heads - 1 - h) * HEAD, step), jnp.bfloat16))
            q_h = jnp.concatenate(pieces, axis=0) if len(pieces) > 1 else q_h
            s_img = dot(k_all[0:img], q_h, NN)
            s_txt = dot(k_all[img:keys], q_h, NN) + bias
            top = jnp.maximum(
                jnp.max(s_img, axis=0, keepdims=True), jnp.max(s_txt, axis=0, keepdims=True)
            )
            p_img = jnp.exp2(s_img - top).astype(jnp.bfloat16)
            p_txt = jnp.exp2(s_txt - top).astype(jnp.bfloat16)
            o = dot(v_s[h, :, 0:img], p_img, NN) + dot(v_s[h, :, img:keys], p_txt, NN)
            o = (o[0:HEAD] / o[HEAD : HEAD + 1]).astype(jnp.bfloat16)
            for i in range(step // rows):
                out_ref[c * (step // rows) + i, h * HEAD : (h + 1) * HEAD, :] = o[
                    :, i * rows : (i + 1) * rows
                ]


def attention(prompt, tokens, mod, bias, w_img, w_txt, seqs, rows):
    block = rows + TXT_PAD
    keys = seqs * block
    width = w_img.shape[1]
    depth = w_img.shape[2]
    heads = width // HEAD
    return pl.pallas_call(
        lambda *refs: attn_kernel(seqs, rows, TXT_PAD, *refs),
        out_shape=jax.ShapeDtypeStruct((seqs, width, rows), jnp.bfloat16),
        grid=(1,),
        in_specs=[
            pl.BlockSpec((1, keys, depth), lambda i: (prompt, 0, 0)),
            pl.BlockSpec((1, 10, depth), lambda i: (prompt, 0, 0)),
            pl.BlockSpec((1, seqs * TXT_PAD, 1), lambda i: (prompt, 0, 0)),
            pl.BlockSpec(w_img.shape, lambda i: (0, 0, 0)),
            pl.BlockSpec(w_txt.shape, lambda i: (0, 0, 0)),
        ],
        out_specs=pl.BlockSpec((seqs, width, rows), lambda i: (0, 0, 0)),
        scratch_shapes=[
            pltpu.VMEM((seqs * rows, depth), jnp.bfloat16),
            pltpu.VMEM((seqs * TXT_PAD, depth), jnp.bfloat16),
            pltpu.VMEM((keys, width), jnp.bfloat16),
            pltpu.VMEM((heads, HEAD + 16, keys), jnp.bfloat16),
            pltpu.VMEM((width, seqs * rows), jnp.bfloat16),
        ],
        compiler_params=pltpu.CompilerParams(vmem_limit_bytes=48 << 20),
        cost_estimate=pl.CostEstimate(flops=1000000, bytes_accessed=1000000, transcendentals=0),
        name="attn",
    )(tokens, mod, bias, w_img, w_txt)


def mlp_kernel(x_ref, up_ref, down_ref, out_ref, acc):
    step = pl.program_id(0)
    depth = up_ref.shape[-1]
    up = up_ref[...].reshape(-1, depth)
    down = down_ref[...].reshape(-1, depth)
    hidden = jax.nn.gelu(dot(x_ref[...], up, NT), approximate=True).astype(jnp.bfloat16)
    term = dot(hidden, down, NN)

    @pl.when(step == 0)
    def _():
        acc[...] = term

    @pl.when(step > 0)
    def _():
        acc[...] += term

    @pl.when(step == pl.num_programs(0) - 1)
    def _():
        out_ref[...] = acc[...].astype(out_ref.dtype)


def mlp(rows_in, weights, out_type):
    shards, _, units, width = weights.shape
    many = 8
    count = rows_in.shape[0]
    return pl.pallas_call(
        mlp_kernel,
        out_shape=jax.ShapeDtypeStruct((count, width), out_type),
        grid=(shards // many,),
        in_specs=[
            pl.BlockSpec((count, width), lambda i: (0, 0)),
            pl.BlockSpec((many, 1, units, width), lambda i: (i, 0, 0, 0)),
            pl.BlockSpec((many, 1, units, width), lambda i: (i, 1, 0, 0)),
        ],
        out_specs=pl.BlockSpec((count, width), lambda i: (0, 0)),
        scratch_shapes=[pltpu.VMEM((count, width), jnp.float32)],
        compiler_params=pltpu.CompilerParams(vmem_limit_bytes=40 << 20),
        cost_estimate=pl.CostEstimate(
            flops=4 * count * shards * units * width,
            bytes_accessed=4 * shards * units * width,
            transcendentals=0,
        ),
        name="mlp",
    )(rows_in, weights, weights)


def swap_cfg(value):
    return lax.ppermute(value, "cfg", [(0, 1), (1, 0)])


def local(
    img_state,
    txt_state,
    cond_vec,
    text_len,
    latent,
    w_mod,
    w_qkv_img,
    w_qkv_txt,
    w_attn_out,
    w_up,
    w_down,
    w_final,
):
    prompts = img_state.shape[1]
    rows = img_state.shape[2]
    width = img_state.shape[3]
    txt_rows = txt_state.shape[2]
    seqs = lax.axis_size("y") * lax.axis_size("core")
    reqs = lax.axis_size("zhi") * lax.axis_size("x")
    everyone = reqs * seqs

    padding = jnp.zeros((prompts, TXT_PAD - txt_rows, width), jnp.bfloat16)
    mine = jnp.concatenate([img_state[0], txt_state[0], padding], axis=1)
    tokens = lax.all_gather(mine, SEQ, axis=1, tiled=True)

    cond_act = jax.nn.silu(cond_vec[0]).astype(jnp.bfloat16)
    part = dot(cond_act, w_mod, NT)
    cols = part.shape[1]
    lanes = -(-cols // 128) * 128
    part = jnp.pad(part, ((0, 0), (0, lanes - cols)))
    part = part.reshape(reqs, 1, prompts * lanes // 128, 128)
    part = jnp.broadcast_to(part, (reqs, seqs) + part.shape[2:]).reshape((everyone,) + part.shape[2:])
    got = lax.all_to_all(part, REQ + SEQ, 0, 0, tiled=True)
    got = got.reshape(everyone, prompts, lanes)[:, :, :cols]
    mod = jnp.swapaxes(got, 0, 1).reshape(prompts, 10, width)

    w_out = lax.all_gather(w_attn_out, SEQ, axis=0, tiled=True)
    weights = lax.all_gather(jnp.stack([w_up, w_down])[None], REQ + SEQ, axis=0, tiled=True)

    slot = jnp.arange(seqs * TXT_PAD)
    inside = slot % TXT_PAD
    index = slot // TXT_PAD * txt_rows + inside
    live = (inside < txt_rows)[None, :] & (index[None, :] < text_len[0][:, None])
    bias = jnp.where(live, 0.0, -1e30).astype(jnp.float32)[:, :, None]

    normed, resid = [], []
    for p in range(prompts):
        att = attention(p, tokens, mod, bias, w_qkv_img, w_qkv_txt, seqs, rows)
        att = lax.all_to_all(att, SEQ, 0, 0, tiled=True).reshape(-1, rows)
        proj = dot(att, w_out, (((0,), (0,)), ((), ())))
        one = (img_state[0, p].astype(jnp.float32) + mod[p, 2] * proj).astype(jnp.bfloat16)
        resid.append(one)
        normed.append(
            (layer_norm(one.astype(jnp.float32)) * (1.0 + mod[p, 4]) + mod[p, 3]).astype(
                jnp.bfloat16
            )
        )
    other = [swap_cfg(n) for n in normed]
    for_other = mlp(jnp.concatenate(other, axis=0), weights, jnp.bfloat16)
    back = swap_cfg(for_other)
    own = mlp(jnp.concatenate(normed, axis=0), weights, jnp.float32)
    mlp_out = (own + back.astype(jnp.float32)).reshape(prompts, rows, width)
    resid_two = jnp.stack(resid).astype(jnp.float32) + mod[:, 5:6] * mlp_out
    final_in = (layer_norm(resid_two) * (1.0 + mod[:, 9:10]) + mod[:, 8:9]).astype(jnp.bfloat16)
    branch_vel = dot(final_in.reshape(prompts * rows, width), w_final, NN)
    branch_vel = branch_vel.reshape(prompts, rows, -1)
    half = latent.shape[2]
    branch = lax.axis_index("cfg")
    first = branch == 0
    low, high = branch_vel[:, :, :half], branch_vel[:, :, half:]
    own_half = jnp.where(first, low, high)
    partner = swap_cfg(jnp.where(first, high, low).astype(jnp.bfloat16)).astype(jnp.float32)
    cond_vel = jnp.where(first, own_half, partner)
    uncond_vel = jnp.where(first, partner, own_half)
    velocity = uncond_vel + 4.5 * (cond_vel - uncond_vel)
    return velocity, latent - 0.04 * velocity


def solution(mesh):
    fine = Mesh(np.asarray(mesh.devices).reshape(2, 2, 4, 4, 2), ("cfg", "zhi", "x", "y", "core"))
    every = ("cfg",) + REQ + SEQ
    placed = (
        P("cfg", REQ, SEQ, None),
        P("cfg", REQ, SEQ, None),
        P("cfg", None, None),
        P("cfg", REQ),
        P(REQ, SEQ, "cfg"),
        P(REQ + SEQ, None),
        P(None, SEQ, None),
        P(None, SEQ, None),
        P(SEQ, None),
        P(every, None),
        P(every, None),
        P(),
    )
    return jax.shard_map(
        local,
        mesh=fine,
        in_specs=placed,
        out_specs=(P(REQ, SEQ, "cfg"), P(REQ, SEQ, "cfg")),
        check_vma=False,
    )
```

```python
import math

import jax
import jax.numpy as jnp
import numpy as np
from jax import lax
from jax.experimental import pallas as pl
from jax.experimental.pallas import tpu as pltpu
from jax.sharding import Mesh
from jax.sharding import PartitionSpec as P

HEAD = 64
SEQ = ("y", "core")
REQ = ("zhi", "x")
NT = (((1,), (1,)), ((), ()))
NN = (((1,), (0,)), ((), ()))
TN = (((0,), (0,)), ((), ()))
TXT_PAD = 32
CHUNK = 32


def dot(a, b, dims):
    return lax.dot_general(a, b, dims, preferred_element_type=jnp.float32)


def layer_norm(value):
    mean = jnp.mean(value, axis=-1, keepdims=True)
    centered = value - mean
    spread = jnp.mean(centered * centered, axis=-1, keepdims=True)
    return centered * lax.rsqrt(spread + 1e-06)


def attn_kernel(idx_ref, *refs):
    *pieces, mod_ref, bias_ref, wi_ref, wt_ref, out_ref, ai, at, k_s, v_s, q_s = refs
    count = len(pieces)
    rows = pieces[0].shape[0] - TXT_PAD
    img = count * rows
    keys = img + count * TXT_PAD

    def modulated(part, scale, shift):
        normed = layer_norm(part.astype(jnp.float32))
        return (normed * (1.0 + mod_ref[0, scale : scale + 1, :]) + mod_ref[0, shift : shift + 1, :]).astype(
            jnp.bfloat16
        )

    for s, piece in enumerate(pieces):

        def one(i, carry, s=s, piece=piece):
            at_row = pl.multiple_of(i * CHUNK, CHUNK)
            ai[pl.ds(pl.multiple_of(s * rows + i * CHUNK, CHUNK), CHUNK), :] = modulated(
                piece[pl.ds(at_row, CHUNK), :], 1, 0
            )
            return carry

        lax.fori_loop(0, rows // CHUNK, one, 0)
        at[s * TXT_PAD : (s + 1) * TXT_PAD, :] = modulated(piece[rows : rows + TXT_PAD, :], 7, 6)
    heads = wi_ref.shape[1] // HEAD
    a_img, a_txt = ai[...], at[...]
    k_s[0:img, :] = dot(a_img, wi_ref[1], NT).astype(jnp.bfloat16)
    k_s[img:keys, :] = dot(a_txt, wt_ref[1], NT).astype(jnp.bfloat16)
    q_s[...] = (dot(wi_ref[0], a_img, NT) * (HEAD ** (-0.5) * math.log2(math.e))).astype(jnp.bfloat16)
    v_img = dot(wi_ref[2], a_img, NT).astype(jnp.bfloat16)
    v_txt = dot(wt_ref[2], a_txt, NT).astype(jnp.bfloat16)
    ones = jnp.ones((16, keys), jnp.bfloat16)
    for h in range(heads):
        v_s[h, 0:HEAD, 0:img] = v_img[h * HEAD : (h + 1) * HEAD, :]
        v_s[h, 0:HEAD, img:keys] = v_txt[h * HEAD : (h + 1) * HEAD, :]
        v_s[h, HEAD : HEAD + 16, :] = ones
    step = 2 * rows

    def some_queries(c, carry):
        at_query = pl.multiple_of(c * step, step)
        for h in range(heads):
            parts = []
            if h:
                parts.append(jnp.zeros((h * HEAD, step), jnp.bfloat16))
            parts.append(q_s[h * HEAD : (h + 1) * HEAD, pl.ds(at_query, step)])
            if h + 1 < heads:
                parts.append(jnp.zeros(((heads - 1 - h) * HEAD, step), jnp.bfloat16))
            q_h = jnp.concatenate(parts, axis=0)
            s_img = dot(k_s[0:img, :], q_h, NN)
            s_txt = dot(k_s[img:keys, :], q_h, NN) + bias_ref[0]
            top = jnp.maximum(
                jnp.max(s_img, axis=0, keepdims=True), jnp.max(s_txt, axis=0, keepdims=True)
            )
            p_img = jnp.exp2(s_img - top).astype(jnp.bfloat16)
            p_txt = jnp.exp2(s_txt - top).astype(jnp.bfloat16)
            o = dot(v_s[h, :, 0:img], p_img, NN) + dot(v_s[h, :, img:keys], p_txt, NN)
            o = (o[0:HEAD] / o[HEAD : HEAD + 1]).astype(jnp.bfloat16)
            for i in range(2):
                out_ref[idx_ref[2 * c + i], h * HEAD : (h + 1) * HEAD, :] = o[:, i * rows : (i + 1) * rows]
        return carry

    lax.fori_loop(0, img // step, some_queries, 0)


def attention(prompt, owners, pieces, mod, bias, w_img, w_txt):
    count = len(pieces)
    block, depth = pieces[0].shape
    rows = block - TXT_PAD
    width = w_img.shape[1]
    heads = width // HEAD
    keys = count * block
    once = lambda *zeros: (lambda i, owners: zeros)
    return pl.pallas_call(
        attn_kernel,
        out_shape=jax.ShapeDtypeStruct((count, width, rows), jnp.bfloat16),
        grid_spec=pltpu.PrefetchScalarGridSpec(
            num_scalar_prefetch=1,
            grid=(1,),
            in_specs=[pl.BlockSpec((block, depth), once(0, 0)) for _ in pieces]
            + [
                pl.BlockSpec((1, 10, depth), once(prompt, 0, 0)),
                pl.BlockSpec((1, count * TXT_PAD, 1), once(prompt, 0, 0)),
                pl.BlockSpec(w_img.shape, once(0, 0, 0)),
                pl.BlockSpec(w_txt.shape, once(0, 0, 0)),
            ],
            out_specs=pl.BlockSpec((count, width, rows), once(0, 0, 0)),
            scratch_shapes=[
                pltpu.VMEM((count * rows, depth), jnp.bfloat16),
                pltpu.VMEM((count * TXT_PAD, depth), jnp.bfloat16),
                pltpu.VMEM((keys, width), jnp.bfloat16),
                pltpu.VMEM((heads, HEAD + 16, keys), jnp.bfloat16),
                pltpu.VMEM((width, count * rows), jnp.bfloat16),
            ],
        ),
        compiler_params=pltpu.CompilerParams(vmem_limit_bytes=48 << 20),
        cost_estimate=pl.CostEstimate(flops=8000000000, bytes_accessed=8000000, transcendentals=0),
        name="attn",
    )(owners, *pieces, mod, bias, w_img, w_txt)


def proj_kernel(idx_ref, att_ref, *refs):
    *parts, img_ref, mod_ref, resid_ref, normed_ref = refs
    total = None
    for s, part in enumerate(parts):
        term = dot(att_ref[idx_ref[s]], part[...], TN)
        total = term if total is None else total + term
    one = (img_ref[0, 0].astype(jnp.float32) + mod_ref[0, 2:3, :] * total).astype(jnp.bfloat16)
    resid_ref[...] = one
    normed = layer_norm(one.astype(jnp.float32)) * (1.0 + mod_ref[0, 4:5, :]) + mod_ref[0, 3:4, :]
    normed_ref[...] = normed.astype(jnp.bfloat16)


def project(prompt, owners, att, parts, img_state, mod):
    rows, depth = img_state.shape[2:]
    once = lambda *zeros: (lambda i, owners: zeros)
    return pl.pallas_call(
        proj_kernel,
        out_shape=[jax.ShapeDtypeStruct((rows, depth), jnp.bfloat16)] * 2,
        grid_spec=pltpu.PrefetchScalarGridSpec(
            num_scalar_prefetch=1,
            grid=(1,),
            in_specs=[pl.BlockSpec(att.shape, once(0, 0, 0))]
            + [pl.BlockSpec(part.shape, once(0, 0)) for part in parts]
            + [
                pl.BlockSpec((1, 1, rows, depth), once(0, prompt, 0, 0)),
                pl.BlockSpec((1, 10, depth), once(prompt, 0, 0)),
            ],
            out_specs=[pl.BlockSpec((rows, depth), once(0, 0))] * 2,
        ),
        compiler_params=pltpu.CompilerParams(vmem_limit_bytes=32 << 20),
        cost_estimate=pl.CostEstimate(flops=600000000, bytes_accessed=5000000, transcendentals=0),
        name="proj",
    )(owners, att, *parts, img_state, mod)


def mlp_kernel(*refs):
    *pieces, up_ref, down_ref, keep_ref, send_ref, x_s, acc = refs
    step = pl.program_id(0)
    depth = up_ref.shape[-1]
    rows = pieces[0].shape[0]

    @pl.when(step == 0)
    def _():
        for i, piece in enumerate(pieces):
            x_s[i * rows : (i + 1) * rows, :] = piece[...]

    up = up_ref[...].reshape(-1, depth)
    down = down_ref[...].reshape(-1, depth)
    hidden = jax.nn.gelu(dot(x_s[...], up, NT), approximate=True).astype(jnp.bfloat16)
    term = dot(hidden, down, NN)

    @pl.when(step == 0)
    def _():
        acc[...] = term

    @pl.when(step > 0)
    def _():
        acc[...] += term

    @pl.when(step == pl.num_programs(0) - 1)
    def _():
        half = keep_ref.shape[0]
        keep_ref[...] = acc[0:half, :]
        send_ref[...] = acc[half:, :].astype(jnp.bfloat16)


def mlp(pieces, weights):
    shards, _, units, width = weights.shape
    many = 8
    rows = pieces[0].shape[0]
    count = rows * len(pieces)
    half = count // 2
    return pl.pallas_call(
        mlp_kernel,
        out_shape=[
            jax.ShapeDtypeStruct((half, width), jnp.float32),
            jax.ShapeDtypeStruct((half, width), jnp.bfloat16),
        ],
        grid=(shards // many,),
        in_specs=[pl.BlockSpec((rows, width), lambda i: (0, 0)) for _ in pieces]
        + [
            pl.BlockSpec((many, 1, units, width), lambda i: (i, 0, 0, 0)),
            pl.BlockSpec((many, 1, units, width), lambda i: (i, 1, 0, 0)),
        ],
        out_specs=[pl.BlockSpec((half, width), lambda i: (0, 0))] * 2,
        scratch_shapes=[
            pltpu.VMEM((count, width), jnp.bfloat16),
            pltpu.VMEM((count, width), jnp.float32),
        ],
        compiler_params=pltpu.CompilerParams(vmem_limit_bytes=44 << 20),
        cost_estimate=pl.CostEstimate(
            flops=4 * count * shards * units * width,
            bytes_accessed=4 * shards * units * width,
            transcendentals=0,
        ),
        name="mlp",
    )(*pieces, weights, weights)


def shifted(value, axis, by):
    size = lax.axis_size(axis)
    return lax.ppermute(value, axis, [(i, (i + by) % size) for i in range(size)])


def swap(value, axis):
    return shifted(value, axis, 1)


def gathered(value, forward_up):
    below = shifted(value, "y", 1)
    above = shifted(value, "y", -1)
    far = shifted(below, "y", 1) if forward_up else shifted(above, "y", -1)
    same = [value, below, above, far]
    return same + [swap(block, "core") for block in same]


def local(
    img_state,
    txt_state,
    cond_vec,
    text_len,
    latent,
    w_mod,
    w_qkv_img,
    w_qkv_txt,
    w_attn_out,
    w_up,
    w_down,
    w_final,
):
    prompts = img_state.shape[1]
    rows = img_state.shape[2]
    width = img_state.shape[3]
    txt_rows = txt_state.shape[2]
    high = lax.axis_size("y")
    seqs = high * lax.axis_size("core")
    reqs = lax.axis_size("zhi") * lax.axis_size("x")
    everyone = reqs * seqs

    own = jnp.stack([w_up, w_down])[None]
    weights = lax.all_gather(
        jnp.concatenate([own, swap(own, "zhi")], axis=0), ("x", "y"), axis=0, tiled=True
    )

    padding = jnp.zeros((prompts, TXT_PAD - txt_rows, width), jnp.bfloat16)
    mine = jnp.concatenate([img_state[0], txt_state[0], padding], axis=1)
    tokens = [gathered(mine[p], p % 2 == 0) for p in range(prompts)]
    w_out = gathered(w_attn_out, True)

    cond_act = jax.nn.silu(cond_vec[0]).astype(jnp.bfloat16)
    part = dot(cond_act, w_mod, NT)
    cols = part.shape[1]
    lanes = -(-cols // 128) * 128
    part = jnp.pad(part, ((0, 0), (0, lanes - cols)))
    part = part.reshape(reqs, 1, prompts * lanes // 128, 128)
    part = jnp.broadcast_to(part, (reqs, seqs) + part.shape[2:]).reshape((everyone,) + part.shape[2:])
    got = lax.all_to_all(part, REQ + SEQ, 0, 0, tiled=True)
    got = got.reshape(everyone, prompts, lanes)[:, :, :cols]
    mod = jnp.swapaxes(got, 0, 1).reshape(prompts, 10, width)

    here, core = lax.axis_index("y"), lax.axis_index("core")
    level = (here + jnp.array([0, high - 1, 1, 2], jnp.int32)) % high
    owners = jnp.concatenate([2 * level + core, 2 * level + 1 - core]).astype(jnp.int32)
    inside = jnp.arange(TXT_PAD)
    index = owners[:, None] * txt_rows + inside[None, :]
    live = (inside < txt_rows)[None, None, :] & (index[None] < text_len[0][:, None, None])
    bias = jnp.where(live, 0.0, -1e30).astype(jnp.float32).reshape(prompts, seqs * TXT_PAD, 1)

    att = [
        attention(p, owners, tokens[p], mod, bias, w_qkv_img, w_qkv_txt) for p in range(prompts)
    ]
    att = [lax.all_to_all(a, SEQ, 0, 0, tiled=True) for a in att]
    resid, normed = zip(
        *[project(p, owners, att[p], w_out, img_state, mod) for p in range(prompts)]
    )
    other = [swap(n, "cfg") for n in normed]
    mate = [swap(n, "core") for n in normed]
    other_mate = [swap(n, "core") for n in other]
    keep, send = mlp(other + other_mate, weights)
    back = swap((keep + swap(send, "core").astype(jnp.float32)).astype(jnp.bfloat16), "cfg")
    keep, send = mlp(list(normed) + mate, weights)
    mlp_out = keep + swap(send, "core").astype(jnp.float32) + back.astype(jnp.float32)
    mlp_out = mlp_out.reshape(prompts, rows, width)
    resid_two = jnp.stack(resid).astype(jnp.float32) + mod[:, 5:6] * mlp_out
    final_in = (layer_norm(resid_two) * (1.0 + mod[:, 9:10]) + mod[:, 8:9]).astype(jnp.bfloat16)
    branch_vel = dot(final_in.reshape(prompts * rows, width), w_final, NN)
    branch_vel = branch_vel.reshape(prompts, rows, -1)
    half = latent.shape[2]
    branch = lax.axis_index("cfg")
    first = branch == 0
    low, upper = branch_vel[:, :, :half], branch_vel[:, :, half:]
    own_half = jnp.where(first, low, upper)
    partner = swap(jnp.where(first, upper, low).astype(jnp.bfloat16), "cfg").astype(jnp.float32)
    cond_vel = jnp.where(first, own_half, partner)
    uncond_vel = jnp.where(first, partner, own_half)
    velocity = uncond_vel + 4.5 * (cond_vel - uncond_vel)
    return velocity, latent - 0.04 * velocity


def solution(mesh):
    fine = Mesh(np.asarray(mesh.devices).reshape(2, 2, 4, 4, 2), ("cfg", "zhi", "x", "y", "core"))
    every = ("cfg",) + REQ + SEQ
    placed = (
        P("cfg", REQ, SEQ, None),
        P("cfg", REQ, SEQ, None),
        P("cfg", None, None),
        P("cfg", REQ),
        P(REQ, SEQ, "cfg"),
        P(REQ + SEQ, None),
        P(None, SEQ, None),
        P(None, SEQ, None),
        P(SEQ, None),
        P(every, None),
        P(every, None),
        P(),
    )
    return jax.shard_map(
        local,
        mesh=fine,
        in_specs=placed,
        out_specs=(P(REQ, SEQ, "cfg"), P(REQ, SEQ, "cfg")),
        check_vma=False,
    )
```

```python
import functools
import math

import jax
import jax.numpy as jnp
import numpy as np
from jax import lax
from jax.experimental import pallas as pl
from jax.experimental.pallas import tpu as pltpu
from jax.sharding import Mesh
from jax.sharding import PartitionSpec as P

HEAD = 64
SEQ = ("y", "core")
REQ = ("zhi", "x")
NT = (((1,), (1,)), ((), ()))
NN = (((1,), (0,)), ((), ()))
TN = (((0,), (0,)), ((), ()))
TXT_PAD = 32


def dot(a, b, dims):
    return lax.dot_general(a, b, dims, preferred_element_type=jnp.float32)


def layer_norm(value):
    mean = jnp.mean(value, axis=-1, keepdims=True)
    centered = value - mean
    spread = jnp.mean(centered * centered, axis=-1, keepdims=True)
    return centered * lax.rsqrt(spread + 1e-06)


def attn_kernel(idx_ref, *refs):
    *pieces, mod_ref, bias_ref, wi_ref, wt_ref, out_ref, ai, at, k_s, v_s, q_s = refs
    count = len(pieces)
    rows = pieces[0].shape[0] - TXT_PAD
    img = count * rows
    keys = img + count * TXT_PAD

    def modulated(part, scale, shift):
        normed = layer_norm(part.astype(jnp.float32))
        return (normed * (1.0 + mod_ref[0, scale : scale + 1, :]) + mod_ref[0, shift : shift + 1, :]).astype(
            jnp.bfloat16
        )

    for s, piece in enumerate(pieces):
        ai[s * rows : (s + 1) * rows, :] = modulated(piece[0:rows, :], 1, 0)
        at[s * TXT_PAD : (s + 1) * TXT_PAD, :] = modulated(piece[rows : rows + TXT_PAD, :], 7, 6)
    heads = wi_ref.shape[1] // HEAD
    a_img, a_txt = ai[...], at[...]
    k_s[0:img, :] = dot(a_img, wi_ref[1], NT).astype(jnp.bfloat16)
    k_s[img:keys, :] = dot(a_txt, wt_ref[1], NT).astype(jnp.bfloat16)
    q_s[...] = (dot(wi_ref[0], a_img, NT) * (HEAD ** (-0.5) * math.log2(math.e))).astype(jnp.bfloat16)
    v_img = dot(wi_ref[2], a_img, NT).astype(jnp.bfloat16)
    v_txt = dot(wt_ref[2], a_txt, NT).astype(jnp.bfloat16)
    ones = jnp.ones((16, keys), jnp.bfloat16)
    for h in range(heads):
        v_s[h, 0:HEAD, 0:img] = v_img[h * HEAD : (h + 1) * HEAD, :]
        v_s[h, 0:HEAD, img:keys] = v_txt[h * HEAD : (h + 1) * HEAD, :]
        v_s[h, HEAD : HEAD + 16, :] = ones
    many = 4
    step = many * rows

    def some_queries(c, carry):
        at_query = pl.multiple_of(c * step, step)
        for h in range(heads):
            parts = []
            if h:
                parts.append(jnp.zeros((h * HEAD, step), jnp.bfloat16))
            parts.append(q_s[h * HEAD : (h + 1) * HEAD, pl.ds(at_query, step)])
            if h + 1 < heads:
                parts.append(jnp.zeros(((heads - 1 - h) * HEAD, step), jnp.bfloat16))
            q_h = jnp.concatenate(parts, axis=0)
            s_img = dot(k_s[0:img, :], q_h, NN)
            s_txt = dot(k_s[img:keys, :], q_h, NN) + bias_ref[0]
            top = jnp.maximum(
                jnp.max(s_img, axis=0, keepdims=True), jnp.max(s_txt, axis=0, keepdims=True)
            )
            p_img = jnp.exp2(s_img - top).astype(jnp.bfloat16)
            p_txt = jnp.exp2(s_txt - top).astype(jnp.bfloat16)
            o = dot(v_s[h, :, 0:img], p_img, NN) + dot(v_s[h, :, img:keys], p_txt, NN)
            o = (o[0:HEAD] / o[HEAD : HEAD + 1]).astype(jnp.bfloat16)
            for i in range(many):
                out_ref[idx_ref[many * c + i], h * HEAD : (h + 1) * HEAD, :] = o[:, i * rows : (i + 1) * rows]
        return carry

    lax.fori_loop(0, img // step, some_queries, 0)


def attention(prompt, owners, pieces, mod, bias, w_img, w_txt):
    count = len(pieces)
    block, depth = pieces[0].shape
    rows = block - TXT_PAD
    width = w_img.shape[1]
    heads = width // HEAD
    keys = count * block
    once = lambda *zeros: (lambda i, owners: zeros)
    return pl.pallas_call(
        attn_kernel,
        out_shape=jax.ShapeDtypeStruct((count, width, rows), jnp.bfloat16),
        grid_spec=pltpu.PrefetchScalarGridSpec(
            num_scalar_prefetch=1,
            grid=(1,),
            in_specs=[pl.BlockSpec((block, depth), once(0, 0)) for _ in pieces]
            + [
                pl.BlockSpec((1, 10, depth), once(prompt, 0, 0)),
                pl.BlockSpec((1, count * TXT_PAD, 1), once(prompt, 0, 0)),
                pl.BlockSpec(w_img.shape, once(0, 0, 0)),
                pl.BlockSpec(w_txt.shape, once(0, 0, 0)),
            ],
            out_specs=pl.BlockSpec((count, width, rows), once(0, 0, 0)),
            scratch_shapes=[
                pltpu.VMEM((count * rows, depth), jnp.bfloat16),
                pltpu.VMEM((count * TXT_PAD, depth), jnp.bfloat16),
                pltpu.VMEM((keys, width), jnp.bfloat16),
                pltpu.VMEM((heads, HEAD + 16, keys), jnp.bfloat16),
                pltpu.VMEM((width, count * rows), jnp.bfloat16),
            ],
        ),
        compiler_params=pltpu.CompilerParams(vmem_limit_bytes=48 << 20),
        cost_estimate=pl.CostEstimate(flops=8000000000, bytes_accessed=8000000, transcendentals=0),
        name="attn",
    )(owners, *pieces, mod, bias, w_img, w_txt)


def proj_kernel(idx_ref, att_ref, *refs):
    *parts, img_ref, mod_ref, resid_ref, normed_ref = refs
    total = None
    for s, part in enumerate(parts):
        term = dot(att_ref[idx_ref[s]], part[...], TN)
        total = term if total is None else total + term
    one = (img_ref[0, 0].astype(jnp.float32) + mod_ref[0, 2:3, :] * total).astype(jnp.bfloat16)
    resid_ref[...] = one
    normed = layer_norm(one.astype(jnp.float32)) * (1.0 + mod_ref[0, 4:5, :]) + mod_ref[0, 3:4, :]
    normed_ref[...] = normed.astype(jnp.bfloat16)


def project(prompt, owners, att, parts, img_state, mod):
    rows, depth = img_state.shape[2:]
    once = lambda *zeros: (lambda i, owners: zeros)
    return pl.pallas_call(
        proj_kernel,
        out_shape=[jax.ShapeDtypeStruct((rows, depth), jnp.bfloat16)] * 2,
        grid_spec=pltpu.PrefetchScalarGridSpec(
            num_scalar_prefetch=1,
            grid=(1,),
            in_specs=[pl.BlockSpec(att.shape, once(0, 0, 0))]
            + [pl.BlockSpec(part.shape, once(0, 0)) for part in parts]
            + [
                pl.BlockSpec((1, 1, rows, depth), once(0, prompt, 0, 0)),
                pl.BlockSpec((1, 10, depth), once(prompt, 0, 0)),
            ],
            out_specs=[pl.BlockSpec((rows, depth), once(0, 0))] * 2,
        ),
        compiler_params=pltpu.CompilerParams(vmem_limit_bytes=32 << 20),
        cost_estimate=pl.CostEstimate(flops=600000000, bytes_accessed=5000000, transcendentals=0),
        name="proj",
    )(owners, att, *parts, img_state, mod)


def mlp_kernel(many_in, *refs):
    pieces = refs[:many_in]
    up_ref, down_ref, keep_ref, *send_refs, x_s, acc = refs[many_in:]
    step = pl.program_id(0)
    depth = up_ref.shape[-1]
    rows = pieces[0].shape[0]

    @pl.when(step == 0)
    def _():
        for i, piece in enumerate(pieces):
            x_s[i * rows : (i + 1) * rows, :] = piece[...]

    up = up_ref[...].reshape(-1, depth)
    down = down_ref[...].reshape(-1, depth)
    hidden = jax.nn.gelu(dot(x_s[...], up, NT), approximate=True).astype(jnp.bfloat16)
    term = dot(hidden, down, NN)

    @pl.when(step == 0)
    def _():
        acc[...] = term

    @pl.when(step > 0)
    def _():
        acc[...] += term

    @pl.when(step == pl.num_programs(0) - 1)
    def _():
        half = keep_ref.shape[0]
        keep_ref[...] = acc[0:half, :]
        cut = send_refs[0].shape[0]
        for i, send_ref in enumerate(send_refs):
            send_ref[...] = acc[half + i * cut : half + (i + 1) * cut, :].astype(jnp.bfloat16)


def mlp(pieces, weights, cuts):
    shards, _, units, width = weights.shape
    many = 8
    rows = pieces[0].shape[0]
    count = rows * len(pieces)
    half = count // 2
    return pl.pallas_call(
        functools.partial(mlp_kernel, len(pieces)),
        out_shape=[jax.ShapeDtypeStruct((half, width), jnp.float32)]
        + [jax.ShapeDtypeStruct((half // cuts, width), jnp.bfloat16)] * cuts,
        grid=(shards // many,),
        in_specs=[pl.BlockSpec((rows, width), lambda i: (0, 0)) for _ in pieces]
        + [
            pl.BlockSpec((many, 1, units, width), lambda i: (i, 0, 0, 0)),
            pl.BlockSpec((many, 1, units, width), lambda i: (i, 1, 0, 0)),
        ],
        out_specs=[pl.BlockSpec((half, width), lambda i: (0, 0))]
        + [pl.BlockSpec((half // cuts, width), lambda i: (0, 0))] * cuts,
        scratch_shapes=[
            pltpu.VMEM((count, width), jnp.bfloat16),
            pltpu.VMEM((count, width), jnp.float32),
        ],
        compiler_params=pltpu.CompilerParams(vmem_limit_bytes=44 << 20),
        cost_estimate=pl.CostEstimate(
            flops=4 * count * shards * units * width,
            bytes_accessed=4 * shards * units * width,
            transcendentals=0,
        ),
        name="mlp",
    )(*pieces, weights, weights)


def finish_kernel(prompts, keep_ref, mod_ref, w_ref, *refs):
    *lists, mine_ref, others_ref = refs
    back, resid, fellow = lists[:prompts], lists[prompts : 2 * prompts], lists[2 * prompts :]
    half = mine_ref.shape[1]
    rows = resid[0].shape[0]
    for p in range(prompts):
        span = slice(p * rows, (p + 1) * rows)
        each = len(fellow) // prompts
        got = jnp.concatenate([part[...] for part in fellow[p * each : (p + 1) * each]], axis=0)
        total = keep_ref[span, :] + got.astype(jnp.float32) + back[p][...].astype(jnp.float32)
        two = resid[p][...].astype(jnp.float32) + mod_ref[p, 5:6, :] * total
        last = layer_norm(two) * (1.0 + mod_ref[p, 9:10, :]) + mod_ref[p, 8:9, :]
        vel = dot(w_ref[...], last.astype(jnp.bfloat16), (((0,), (1,)), ((), ())))
        mine_ref[p] = vel[0:half]
        others_ref[p] = vel[half:].astype(jnp.bfloat16)


def finish(keep, fellow, back, resid, mod, w_last):
    prompts = len(back)
    rows = back[0].shape[0]
    half = w_last.shape[1] // 2
    shape = (prompts, half, rows)
    return pl.pallas_call(
        functools.partial(finish_kernel, prompts),
        out_shape=[jax.ShapeDtypeStruct(shape, jnp.float32), jax.ShapeDtypeStruct(shape, jnp.bfloat16)],
        compiler_params=pltpu.CompilerParams(vmem_limit_bytes=32 << 20),
        name="finish",
    )(keep, mod, w_last, *back, *resid, *fellow)


def shifted(value, axis, by):
    size = lax.axis_size(axis)
    return lax.ppermute(value, axis, [(i, (i + by) % size) for i in range(size)])


def swap(value, axis):
    return shifted(value, axis, 1)


def gathered(value, forward_up):
    below = shifted(value, "y", 1)
    above = shifted(value, "y", -1)
    far = shifted(below, "y", 1) if forward_up else shifted(above, "y", -1)
    same = [value, below, above, far]
    return same + [swap(block, "core") for block in same]


def local(
    img_state,
    txt_state,
    cond_vec,
    text_len,
    latent,
    w_mod,
    w_qkv_img,
    w_qkv_txt,
    w_attn_out,
    w_up,
    w_down,
    w_final,
):
    prompts = img_state.shape[1]
    rows = img_state.shape[2]
    width = img_state.shape[3]
    txt_rows = txt_state.shape[2]
    high = lax.axis_size("y")
    seqs = high * lax.axis_size("core")
    reqs = lax.axis_size("zhi") * lax.axis_size("x")
    everyone = reqs * seqs

    own = jnp.stack([w_up, w_down])[None]
    weights = lax.all_gather(
        jnp.concatenate([own, swap(own, "zhi")], axis=0), ("x", "y"), axis=0, tiled=True
    )

    padding = jnp.zeros((prompts, TXT_PAD - txt_rows, width), jnp.bfloat16)
    mine = jnp.concatenate([img_state[0], txt_state[0], padding], axis=1)
    tokens = [gathered(mine[p], p % 2 == 0) for p in range(prompts)]
    later, _ = lax.optimization_barrier((w_attn_out, tokens[-1][3]))
    w_out = gathered(later, True)

    cond_act = jax.nn.silu(cond_vec[0]).astype(jnp.bfloat16)
    part = dot(cond_act, w_mod, NT)
    cols = part.shape[1]
    lanes = -(-cols // 128) * 128
    part = jnp.pad(part, ((0, 0), (0, lanes - cols)))
    part = part.reshape(reqs, 1, prompts * lanes // 128, 128)
    part = jnp.broadcast_to(part, (reqs, seqs) + part.shape[2:]).reshape((everyone,) + part.shape[2:])
    got = lax.all_to_all(part, REQ + SEQ, 0, 0, tiled=True)
    got = got.reshape(everyone, prompts, lanes)[:, :, :cols]
    mod = jnp.swapaxes(got, 0, 1).reshape(prompts, 10, width)

    here, core = lax.axis_index("y"), lax.axis_index("core")
    level = (here + jnp.array([0, high - 1, 1, 2], jnp.int32)) % high
    owners = jnp.concatenate([2 * level + core, 2 * level + 1 - core]).astype(jnp.int32)
    inside = jnp.arange(TXT_PAD)
    index = owners[:, None] * txt_rows + inside[None, :]
    live = (inside < txt_rows)[None, None, :] & (index[None] < text_len[0][:, None, None])
    bias = jnp.where(live, 0.0, -1e30).astype(jnp.float32).reshape(prompts, seqs * TXT_PAD, 1)

    att = [
        attention(p, owners, tokens[p], mod, bias, w_qkv_img, w_qkv_txt) for p in range(prompts)
    ]
    last = att[-1]
    att = [lax.all_to_all(a, SEQ, 0, 0, tiled=True) for a in att]
    att[0], _ = lax.optimization_barrier((att[0], last))
    resid, normed = zip(
        *[project(p, owners, att[p], w_out, img_state, mod) for p in range(prompts)]
    )
    other = [swap(n, "cfg") for n in normed]
    mate = [swap(n, "core") for n in normed]
    other_mate = [swap(n, "core") for n in other]
    other, other_mate, mate = lax.optimization_barrier((other, other_mate, mate))
    back = []
    for p in range(prompts):
        rows_in = [other[p], other_mate[p]]
        if back:
            rows_in, back[-1] = lax.optimization_barrier((rows_in, back[-1]))
        keep, *send = mlp(rows_in, weights, 2)
        got = jnp.concatenate([swap(part, "core") for part in send], axis=0)
        back.append((keep + got.astype(jnp.float32)).astype(jnp.bfloat16))
    rows_in, back[-1] = lax.optimization_barrier((list(normed) + mate, back[-1]))
    back = [swap(b, "cfg") for b in back]
    keep, *send = mlp(rows_in, weights, 4)
    fellow = [swap(part, "core") for part in send]

    half = latent.shape[2]
    branch = lax.axis_index("cfg")
    first = branch == 0
    w_last = jnp.where(first, w_final, jnp.concatenate([w_final[:, half:], w_final[:, :half]], axis=1))
    mine, others = finish(keep, fellow, back, resid, mod, w_last)
    partner = swap(others, "cfg").astype(jnp.float32)
    cond_vel = jnp.where(first, mine, partner)
    uncond_vel = jnp.where(first, partner, mine)
    velocity = uncond_vel + 4.5 * (cond_vel - uncond_vel)
    latent_next = jnp.swapaxes(latent, 1, 2) - 0.04 * velocity
    return jnp.swapaxes(velocity, 1, 2), jnp.swapaxes(latent_next, 1, 2)


def solution(mesh):
    fine = Mesh(np.asarray(mesh.devices).reshape(2, 2, 4, 4, 2), ("cfg", "zhi", "x", "y", "core"))
    every = ("cfg",) + REQ + SEQ
    placed = (
        P("cfg", REQ, SEQ, None),
        P("cfg", REQ, SEQ, None),
        P("cfg", None, None),
        P("cfg", REQ),
        P(REQ, SEQ, "cfg"),
        P(REQ + SEQ, None),
        P(None, SEQ, None),
        P(None, SEQ, None),
        P(SEQ, None),
        P(every, None),
        P(every, None),
        P(),
    )
    return jax.shard_map(
        local,
        mesh=fine,
        in_specs=placed,
        out_specs=(P(REQ, SEQ, "cfg"), P(REQ, SEQ, "cfg")),
        check_vma=False,
    )
```

```python
import functools
import math

import jax
import jax.numpy as jnp
import numpy as np
from jax import lax
from jax.experimental import pallas as pl
from jax.experimental.pallas import tpu as pltpu
from jax.sharding import Mesh
from jax.sharding import PartitionSpec as P

HEAD = 64
SEQ = ("y", "core")
REQ = ("zhi", "x")
NT = (((1,), (1,)), ((), ()))
NN = (((1,), (0,)), ((), ()))
TN = (((0,), (0,)), ((), ()))
TXT_PAD = 32


def dot(a, b, dims):
    return lax.dot_general(a, b, dims, preferred_element_type=jnp.float32)


def layer_norm(value):
    mean = jnp.mean(value, axis=-1, keepdims=True)
    centered = value - mean
    spread = jnp.mean(centered * centered, axis=-1, keepdims=True)
    return centered * lax.rsqrt(spread + 1e-06)


def attn_kernel(idx_ref, *refs):
    *pieces, mod_ref, bias_ref, wi_ref, wt_ref, out_ref, ai, at, k_s, v_s, q_s = refs
    count = len(pieces)
    rows = pieces[0].shape[0] - TXT_PAD
    img = count * rows
    keys = img + count * TXT_PAD

    def modulated(part, scale, shift):
        normed = layer_norm(part.astype(jnp.float32))
        return (normed * (1.0 + mod_ref[0, scale : scale + 1, :]) + mod_ref[0, shift : shift + 1, :]).astype(
            jnp.bfloat16
        )

    for s, piece in enumerate(pieces):
        ai[s * rows : (s + 1) * rows, :] = modulated(piece[0:rows, :], 1, 0)
        at[s * TXT_PAD : (s + 1) * TXT_PAD, :] = modulated(piece[rows : rows + TXT_PAD, :], 7, 6)
    heads = wi_ref.shape[1] // HEAD
    a_img, a_txt = ai[...], at[...]
    k_s[0:img, :] = dot(a_img, wi_ref[1], NT).astype(jnp.bfloat16)
    k_s[img:keys, :] = dot(a_txt, wt_ref[1], NT).astype(jnp.bfloat16)
    q_s[...] = (dot(wi_ref[0], a_img, NT) * (HEAD ** (-0.5) * math.log2(math.e))).astype(jnp.bfloat16)
    v_img = dot(wi_ref[2], a_img, NT).astype(jnp.bfloat16)
    v_txt = dot(wt_ref[2], a_txt, NT).astype(jnp.bfloat16)
    ones = jnp.ones((16, keys), jnp.bfloat16)
    for h in range(heads):
        v_s[h, 0:HEAD, 0:img] = v_img[h * HEAD : (h + 1) * HEAD, :]
        v_s[h, 0:HEAD, img:keys] = v_txt[h * HEAD : (h + 1) * HEAD, :]
        v_s[h, HEAD : HEAD + 16, :] = ones
    many = 4
    step = many * rows

    def some_queries(c, carry):
        at_query = pl.multiple_of(c * step, step)
        for h in range(heads):
            parts = []
            if h:
                parts.append(jnp.zeros((h * HEAD, step), jnp.bfloat16))
            parts.append(q_s[h * HEAD : (h + 1) * HEAD, pl.ds(at_query, step)])
            if h + 1 < heads:
                parts.append(jnp.zeros(((heads - 1 - h) * HEAD, step), jnp.bfloat16))
            q_h = jnp.concatenate(parts, axis=0)
            s_img = dot(k_s[0:img, :], q_h, NN)
            s_txt = dot(k_s[img:keys, :], q_h, NN) + bias_ref[0]
            top = jnp.maximum(
                jnp.max(s_img, axis=0, keepdims=True), jnp.max(s_txt, axis=0, keepdims=True)
            )
            p_img = jnp.exp2(s_img - top).astype(jnp.bfloat16)
            p_txt = jnp.exp2(s_txt - top).astype(jnp.bfloat16)
            o = dot(v_s[h, :, 0:img], p_img, NN) + dot(v_s[h, :, img:keys], p_txt, NN)
            o = (o[0:HEAD] / o[HEAD : HEAD + 1]).astype(jnp.bfloat16)
            for i in range(many):
                out_ref[idx_ref[many * c + i], h * HEAD : (h + 1) * HEAD, :] = o[:, i * rows : (i + 1) * rows]
        return carry

    lax.fori_loop(0, img // step, some_queries, 0)


def attention(prompt, owners, pieces, mod, bias, w_img, w_txt):
    count = len(pieces)
    block, depth = pieces[0].shape
    rows = block - TXT_PAD
    width = w_img.shape[1]
    heads = width // HEAD
    keys = count * block
    once = lambda *zeros: (lambda i, owners: zeros)
    return pl.pallas_call(
        attn_kernel,
        out_shape=jax.ShapeDtypeStruct((count, width, rows), jnp.bfloat16),
        grid_spec=pltpu.PrefetchScalarGridSpec(
            num_scalar_prefetch=1,
            grid=(1,),
            in_specs=[pl.BlockSpec((block, depth), once(0, 0)) for _ in pieces]
            + [
                pl.BlockSpec((1, 10, depth), once(prompt, 0, 0)),
                pl.BlockSpec((1, count * TXT_PAD, 1), once(prompt, 0, 0)),
                pl.BlockSpec(w_img.shape, once(0, 0, 0)),
                pl.BlockSpec(w_txt.shape, once(0, 0, 0)),
            ],
            out_specs=pl.BlockSpec((count, width, rows), once(0, 0, 0)),
            scratch_shapes=[
                pltpu.VMEM((count * rows, depth), jnp.bfloat16),
                pltpu.VMEM((count * TXT_PAD, depth), jnp.bfloat16),
                pltpu.VMEM((keys, width), jnp.bfloat16),
                pltpu.VMEM((heads, HEAD + 16, keys), jnp.bfloat16),
                pltpu.VMEM((width, count * rows), jnp.bfloat16),
            ],
        ),
        compiler_params=pltpu.CompilerParams(vmem_limit_bytes=48 << 20),
        cost_estimate=pl.CostEstimate(flops=8000000000, bytes_accessed=8000000, transcendentals=0),
        name="attn",
    )(owners, *pieces, mod, bias, w_img, w_txt)


def proj_kernel(att_ref, w_ref, img_ref, mod_ref, resid_ref, normed_ref):
    total = dot(att_ref[...], w_ref[...], TN)
    one = (img_ref[0, 0].astype(jnp.float32) + mod_ref[0, 2:3, :] * total).astype(jnp.bfloat16)
    resid_ref[...] = one
    normed = layer_norm(one.astype(jnp.float32)) * (1.0 + mod_ref[0, 4:5, :]) + mod_ref[0, 3:4, :]
    normed_ref[...] = normed.astype(jnp.bfloat16)


def project(prompt, att, w_out, img_state, mod):
    rows, depth = img_state.shape[2:]
    return pl.pallas_call(
        proj_kernel,
        out_shape=[jax.ShapeDtypeStruct((rows, depth), jnp.bfloat16)] * 2,
        grid=(1,),
        in_specs=[
            pl.BlockSpec(att.shape, lambda i: (0, 0)),
            pl.BlockSpec(w_out.shape, lambda i: (0, 0)),
            pl.BlockSpec((1, 1, rows, depth), lambda i: (0, prompt, 0, 0)),
            pl.BlockSpec((1, 10, depth), lambda i: (prompt, 0, 0)),
        ],
        out_specs=[pl.BlockSpec((rows, depth), lambda i: (0, 0))] * 2,
        compiler_params=pltpu.CompilerParams(vmem_limit_bytes=32 << 20),
        cost_estimate=pl.CostEstimate(flops=600000000, bytes_accessed=5000000, transcendentals=0),
        name="proj",
    )(att, w_out, img_state, mod)


def mlp_kernel(*refs):
    many = (len(refs) - 4) // 2
    pieces, (up_ref, down_ref), outs, (x_s, acc) = refs[:many], refs[many : many + 2], refs[many + 2 : -2], refs[-2:]
    step = pl.program_id(0)
    depth = up_ref.shape[-1]
    rows = pieces[0].shape[0]

    @pl.when(step == 0)
    def _():
        for i, piece in enumerate(pieces):
            x_s[i * rows : (i + 1) * rows, :] = piece[...]

    up = up_ref[...].reshape(-1, depth)
    down = down_ref[...].reshape(-1, depth)
    hidden = jax.nn.gelu(dot(x_s[...], up, NT), approximate=True).astype(jnp.bfloat16)
    term = dot(hidden, down, NN)

    @pl.when(step == 0)
    def _():
        acc[...] = term

    @pl.when(step > 0)
    def _():
        acc[...] += term

    @pl.when(step == pl.num_programs(0) - 1)
    def _():
        for i, out in enumerate(outs):
            out[...] = acc[i * rows : (i + 1) * rows, :].astype(out.dtype)


def mlp(pieces, types, weights):
    shards, _, units, width = weights.shape
    many = 8
    rows = pieces[0].shape[0]
    count = rows * len(pieces)
    return pl.pallas_call(
        mlp_kernel,
        out_shape=[jax.ShapeDtypeStruct((rows, width), t) for t in types],
        grid=(shards // many,),
        in_specs=[pl.BlockSpec((rows, width), lambda i: (0, 0)) for _ in pieces]
        + [
            pl.BlockSpec((many, 1, units, width), lambda i: (i, 0, 0, 0)),
            pl.BlockSpec((many, 1, units, width), lambda i: (i, 1, 0, 0)),
        ],
        out_specs=[pl.BlockSpec((rows, width), lambda i: (0, 0))] * len(types),
        scratch_shapes=[
            pltpu.VMEM((count, width), jnp.bfloat16),
            pltpu.VMEM((count, width), jnp.float32),
        ],
        compiler_params=pltpu.CompilerParams(vmem_limit_bytes=44 << 20),
        cost_estimate=pl.CostEstimate(
            flops=4 * count * shards * units * width,
            bytes_accessed=4 * shards * units * width,
            transcendentals=0,
        ),
        name="mlp",
    )(*pieces, weights, weights)


def finish_kernel(prompts, mod_ref, w_ref, *refs):
    *lists, mine_ref, others_ref = refs
    half = mine_ref.shape[1]
    each = len(lists) // prompts
    for p in range(prompts):
        resid, *terms = lists[p * each : (p + 1) * each]
        total = terms[0][...].astype(jnp.float32)
        for term in terms[1:]:
            total = total + term[...].astype(jnp.float32)
        two = resid[...].astype(jnp.float32) + mod_ref[p, 5:6, :] * total
        last = layer_norm(two) * (1.0 + mod_ref[p, 9:10, :]) + mod_ref[p, 8:9, :]
        vel = dot(w_ref[...], last.astype(jnp.bfloat16), (((0,), (1,)), ((), ())))
        mine_ref[p] = vel[0:half]
        others_ref[p] = vel[half:].astype(jnp.bfloat16)


def finish(lists, mod, w_last):
    prompts = len(lists)
    half = w_last.shape[1] // 2
    shape = (prompts, half, lists[0][0].shape[0])
    return pl.pallas_call(
        functools.partial(finish_kernel, prompts),
        out_shape=[jax.ShapeDtypeStruct(shape, jnp.float32), jax.ShapeDtypeStruct(shape, jnp.bfloat16)],
        compiler_params=pltpu.CompilerParams(vmem_limit_bytes=32 << 20),
        name="finish",
    )(mod, w_last, *[value for one in lists for value in one])


def shifted(value, axis, by):
    size = lax.axis_size(axis)
    return lax.ppermute(value, axis, [(i, (i + by) % size) for i in range(size)])


def swap(value, axis):
    return shifted(value, axis, 1)


def along_z(value, by):
    place = lambda z: z % 2 * 2 + z // 2
    pairs = [(place(z), place((z + by) % 4)) for z in range(4)]
    return lax.ppermute(value, ("cfg", "zhi"), pairs)


def local(
    img_state,
    txt_state,
    cond_vec,
    text_len,
    latent,
    w_mod,
    w_qkv_img,
    w_qkv_txt,
    w_attn_out,
    w_up,
    w_down,
    w_final,
):
    prompts = img_state.shape[1]
    rows = img_state.shape[2]
    width = img_state.shape[3]
    txt_rows = txt_state.shape[2]
    high = lax.axis_size("y")
    seqs = high * lax.axis_size("core")
    reqs = lax.axis_size("zhi") * lax.axis_size("x")
    everyone = reqs * seqs

    padding = jnp.zeros((prompts, TXT_PAD - txt_rows, width), jnp.bfloat16)
    mine = jnp.concatenate([img_state[0], txt_state[0], padding], axis=1)
    below = shifted(mine, "y", 1)
    above = shifted(mine, "y", -1)
    far = [shifted(below[p], "y", 1) if p % 2 == 0 else shifted(above[p], "y", -1) for p in range(prompts)]
    pairs = [mine, below, above]
    mates = [swap(block, "core") for block in pairs]
    tokens = [
        [block[p] for block in pairs] + [far[p]] + [block[p] for block in mates] + [swap(far[p], "core")]
        for p in range(prompts)
    ]

    w_out = lax.all_gather(w_attn_out, SEQ, axis=0, tiled=True)
    weights = lax.all_gather(
        jnp.stack([w_up, w_down])[None], ("x",) + SEQ, axis=0, tiled=True
    )

    cond_act = jax.nn.silu(cond_vec[0]).astype(jnp.bfloat16)
    part = dot(cond_act, w_mod, NT)
    cols = part.shape[1]
    lanes = -(-cols // 128) * 128
    part = jnp.pad(part, ((0, 0), (0, lanes - cols)))
    part = part.reshape(reqs, 1, prompts * lanes // 128, 128)
    part = jnp.broadcast_to(part, (reqs, seqs) + part.shape[2:]).reshape((everyone,) + part.shape[2:])
    got = lax.all_to_all(part, REQ + SEQ, 0, 0, tiled=True)
    got = got.reshape(everyone, prompts, lanes)[:, :, :cols]
    mod = jnp.swapaxes(got, 0, 1).reshape(prompts, 10, width)

    here, core = lax.axis_index("y"), lax.axis_index("core")
    level = (here + jnp.array([0, high - 1, 1, 2], jnp.int32)) % high
    owners = jnp.concatenate([2 * level + core, 2 * level + 1 - core]).astype(jnp.int32)
    inside = jnp.arange(TXT_PAD)
    index = owners[:, None] * txt_rows + inside[None, :]
    live = (inside < txt_rows)[None, None, :] & (index[None] < text_len[0][:, None, None])
    bias = jnp.where(live, 0.0, -1e30).astype(jnp.float32).reshape(prompts, seqs * TXT_PAD, 1)

    att = [
        attention(p, owners, tokens[p], mod, bias, w_qkv_img, w_qkv_txt) for p in range(prompts)
    ]
    last = att[-1]
    att = [lax.all_to_all(a, SEQ, 0, 0, tiled=True) for a in att]
    att[0], _ = lax.optimization_barrier((att[0], last))
    resid, normed = zip(
        *[
            project(p, att[p].reshape(-1, rows), w_out, img_state, mod)
            for p in range(prompts)
        ]
    )
    low = [along_z(n, 1) for n in normed]
    high_rows = [along_z(n, -1) for n in normed]
    away = [along_z(low[0], 1), along_z(high_rows[1], -1)]
    f32, bf16 = jnp.float32, jnp.bfloat16
    hop0, hop1 = mlp(away, [bf16, bf16], weights)
    near = [low[0], high_rows[1], high_rows[0], low[1]]
    near, _ = lax.optimization_barrier((near, hop0))
    low0, high1, high0, low1 = mlp(near, [bf16, bf16, f32, f32], weights)
    hop0, hop1 = along_z(hop0, 1), along_z(hop1, -1)
    terms = [
        [along_z(low0, -1), along_z((high0 + hop0.astype(f32)).astype(bf16), 1)],
        [along_z(high1, 1), along_z((low1 + hop1.astype(f32)).astype(bf16), -1)],
    ]
    own, _ = lax.optimization_barrier((list(normed), low0))
    own = mlp(own, [f32, f32], weights)
    lists = [[resid[p], own[p]] + terms[p] for p in range(prompts)]

    half = latent.shape[2]
    branch = lax.axis_index("cfg")
    first = branch == 0
    w_last = jnp.where(first, w_final, jnp.concatenate([w_final[:, half:], w_final[:, :half]], axis=1))
    mine, others = finish(lists, mod, w_last)
    partner = swap(others, "cfg").astype(jnp.float32)
    cond_vel = jnp.where(first, mine, partner)
    uncond_vel = jnp.where(first, partner, mine)
    velocity = uncond_vel + 4.5 * (cond_vel - uncond_vel)
    latent_next = jnp.swapaxes(latent, 1, 2) - 0.04 * velocity
    return jnp.swapaxes(velocity, 1, 2), jnp.swapaxes(latent_next, 1, 2)


def solution(mesh):
    fine = Mesh(np.asarray(mesh.devices).reshape(2, 2, 4, 4, 2), ("cfg", "zhi", "x", "y", "core"))
    every = ("cfg",) + REQ + SEQ
    placed = (
        P("cfg", REQ, SEQ, None),
        P("cfg", REQ, SEQ, None),
        P("cfg", None, None),
        P("cfg", REQ),
        P(REQ, SEQ, "cfg"),
        P(REQ + SEQ, None),
        P(None, SEQ, None),
        P(None, SEQ, None),
        P(SEQ, None),
        P(every, None),
        P(every, None),
        P(),
    )
    return jax.shard_map(
        local,
        mesh=fine,
        in_specs=placed,
        out_specs=(P(REQ, SEQ, "cfg"), P(REQ, SEQ, "cfg")),
        check_vma=False,
    )
```

```python
import functools
import math

import jax
import jax.numpy as jnp
import numpy as np
from jax import lax
from jax.experimental import pallas as pl
from jax.experimental.pallas import tpu as pltpu
from jax.sharding import Mesh
from jax.sharding import PartitionSpec as P

HEAD = 64
SEQ = ("y", "core")
REQ = ("zhi", "x")
NT = (((1,), (1,)), ((), ()))
NN = (((1,), (0,)), ((), ()))
TN = (((0,), (0,)), ((), ()))
TXT_PAD = 32


def dot(a, b, dims):
    return lax.dot_general(a, b, dims, preferred_element_type=jnp.float32)


def layer_norm(value):
    mean = jnp.mean(value, axis=-1, keepdims=True)
    centered = value - mean
    spread = jnp.mean(centered * centered, axis=-1, keepdims=True)
    return centered * lax.rsqrt(spread + 1e-06)


def attn_kernel(prompt, many, idx_ref, *refs):
    pieces = refs[:many]
    mod_ref, bias_ref, wi_ref, wt_ref, out_ref, x_s, wi_s, wt_s, ai, at, k_s, v_s, q_s, x_sem, w_sem = refs[many:]
    block = x_s.shape[1]
    rows = block - TXT_PAD
    img = many * rows
    keys = many * block
    width = wt_s.shape[0] // 2
    heads = width // HEAD

    def take(s):
        piece = pieces[s] if len(pieces[s].shape) == 2 else pieces[s].at[prompt]
        return pltpu.make_async_copy(piece, x_s.at[s], x_sem.at[s])

    order = [(wi_ref, 0, wi_s, 0), (wi_ref, 2, wi_s, 1), (wi_ref, 1, wi_s, 2), (wt_ref, 2, wt_s, 0), (wt_ref, 1, wt_s, 1)]
    loads = [
        pltpu.make_async_copy(src.at[j], dst.at[pl.ds(i * width, width)], w_sem.at[n])
        for n, (src, j, dst, i) in enumerate(order)
    ]
    for s in range(many):
        take(s).start()
    for load in loads:
        load.start()

    def modulated(part, scale, shift):
        normed = layer_norm(part.astype(jnp.float32))
        return (normed * (1.0 + mod_ref[0, scale : scale + 1, :]) + mod_ref[0, shift : shift + 1, :]).astype(
            jnp.bfloat16
        )

    for s in range(many):
        take(s).wait()

    def one_piece(s, carry):
        ai[pl.ds(pl.multiple_of(s * rows, rows), rows), :] = modulated(x_s[s, 0:rows, :], 1, 0)
        at[pl.ds(pl.multiple_of(s * TXT_PAD, TXT_PAD), TXT_PAD), :] = modulated(x_s[s, rows:block, :], 7, 6)
        return carry

    lax.fori_loop(0, many, one_piece, 0)
    for load in loads:
        load.wait()
    ones = jnp.ones((16, keys), jnp.bfloat16)
    for h in range(heads):
        v_s[h, HEAD : HEAD + 16, :] = ones
    wide = 2 * rows

    def some_rows(c, carry):
        span = pl.ds(pl.multiple_of(c * wide, wide), wide)
        a = ai[span, :]
        k_s[span, :] = dot(a, wi_s[2 * width : 3 * width, :], NT).astype(jnp.bfloat16)
        both = dot(wi_s[0 : 2 * width, :], a, NT)
        q_s[:, span] = (both[0:width] * (HEAD ** (-0.5) * math.log2(math.e))).astype(jnp.bfloat16)
        for h in range(heads):
            v_s[h, 0:HEAD, span] = both[width + h * HEAD : width + (h + 1) * HEAD].astype(jnp.bfloat16)
        return carry

    lax.fori_loop(0, img // wide, some_rows, 0)
    a_txt = at[...]
    k_s[img:keys, :] = dot(a_txt, wt_s[width : 2 * width, :], NT).astype(jnp.bfloat16)
    v_txt = dot(wt_s[0:width, :], a_txt, NT).astype(jnp.bfloat16)
    for h in range(heads):
        v_s[h, 0:HEAD, img:keys] = v_txt[h * HEAD : (h + 1) * HEAD, :]
    held = 4
    step = held * rows

    def some_queries(c, carry):
        at_query = pl.multiple_of(c * step, step)
        for h in range(heads):
            parts = []
            if h:
                parts.append(jnp.zeros((h * HEAD, step), jnp.bfloat16))
            parts.append(q_s[h * HEAD : (h + 1) * HEAD, pl.ds(at_query, step)])
            if h + 1 < heads:
                parts.append(jnp.zeros(((heads - 1 - h) * HEAD, step), jnp.bfloat16))
            q_h = jnp.concatenate(parts, axis=0)
            s_img = dot(k_s[0:img, :], q_h, NN)
            s_txt = dot(k_s[img:keys, :], q_h, NN) + bias_ref[0]
            top = jnp.maximum(
                jnp.max(s_img, axis=0, keepdims=True), jnp.max(s_txt, axis=0, keepdims=True)
            )
            p_img = jnp.exp2(s_img - top).astype(jnp.bfloat16)
            p_txt = jnp.exp2(s_txt - top).astype(jnp.bfloat16)
            o = dot(v_s[h, :, 0:img], p_img, NN) + dot(v_s[h, :, img:keys], p_txt, NN)
            o = (o[0:HEAD] / o[HEAD : HEAD + 1]).astype(jnp.bfloat16)
            for i in range(held):
                out_ref[idx_ref[held * c + i], h * HEAD : (h + 1) * HEAD, :] = o[:, i * rows : (i + 1) * rows]
        return carry

    lax.fori_loop(0, img // step, some_queries, 0)


def attention(prompt, owners, pieces, mod, bias, w_img, w_txt):
    many = len(pieces)
    block, depth = pieces[0].shape[-2:]
    rows = block - TXT_PAD
    width = w_img.shape[1]
    heads = width // HEAD
    keys = many * block
    once = lambda *zeros: (lambda i, owners: zeros)
    stays = pl.BlockSpec(memory_space=pltpu.HBM)
    bf16 = jnp.bfloat16
    return pl.pallas_call(
        functools.partial(attn_kernel, prompt, many),
        out_shape=jax.ShapeDtypeStruct((many, width, rows), bf16),
        grid_spec=pltpu.PrefetchScalarGridSpec(
            num_scalar_prefetch=1,
            grid=(1,),
            in_specs=[stays] * many
            + [
                pl.BlockSpec((1, 10, depth), once(prompt, 0, 0)),
                pl.BlockSpec((1, many * TXT_PAD, 1), once(prompt, 0, 0)),
                stays,
                stays,
            ],
            out_specs=pl.BlockSpec((many, width, rows), once(0, 0, 0)),
            scratch_shapes=[
                pltpu.VMEM((many, block, depth), bf16),
                pltpu.VMEM((3 * width, depth), bf16),
                pltpu.VMEM((2 * width, depth), bf16),
                pltpu.VMEM((many * rows, depth), bf16),
                pltpu.VMEM((many * TXT_PAD, depth), bf16),
                pltpu.VMEM((keys, width), bf16),
                pltpu.VMEM((heads, HEAD + 16, keys), bf16),
                pltpu.VMEM((width, many * rows), bf16),
                pltpu.SemaphoreType.DMA((many,)),
                pltpu.SemaphoreType.DMA((5,)),
            ],
        ),
        compiler_params=pltpu.CompilerParams(vmem_limit_bytes=56 << 20),
        cost_estimate=pl.CostEstimate(flops=8000000000, bytes_accessed=8000000, transcendentals=0),
        name="attn",
    )(owners, *pieces, mod, bias, w_img, w_txt)


def proj_kernel(many, idx_ref, att_ref, *refs):
    parts = refs[:many]
    img_ref, mod_ref, resid_ref, normed_ref, w_s, sem = refs[many:]
    loads = [pltpu.make_async_copy(part, w_s.at[s], sem.at[s]) for s, part in enumerate(parts)]
    for load in loads:
        load.start()
    total = None
    for s, load in enumerate(loads):
        load.wait()
        term = dot(att_ref[idx_ref[s]], w_s[s], TN)
        total = term if total is None else total + term
    one = (img_ref[0, 0].astype(jnp.float32) + mod_ref[0, 2:3, :] * total).astype(jnp.bfloat16)
    resid_ref[...] = one
    normed = layer_norm(one.astype(jnp.float32)) * (1.0 + mod_ref[0, 4:5, :]) + mod_ref[0, 3:4, :]
    normed_ref[...] = normed.astype(jnp.bfloat16)


def project(prompt, owners, att, parts, img_state, mod):
    rows, depth = img_state.shape[2:]
    many = len(parts)
    once = lambda *zeros: (lambda i, owners: zeros)
    return pl.pallas_call(
        functools.partial(proj_kernel, many),
        out_shape=[jax.ShapeDtypeStruct((rows, depth), jnp.bfloat16)] * 2,
        grid_spec=pltpu.PrefetchScalarGridSpec(
            num_scalar_prefetch=1,
            grid=(1,),
            in_specs=[pl.BlockSpec(att.shape, once(0, 0, 0))]
            + [pl.BlockSpec(memory_space=pltpu.HBM)] * many
            + [
                pl.BlockSpec((1, 1, rows, depth), once(0, prompt, 0, 0)),
                pl.BlockSpec((1, 10, depth), once(prompt, 0, 0)),
            ],
            out_specs=[pl.BlockSpec((rows, depth), once(0, 0))] * 2,
            scratch_shapes=[
                pltpu.VMEM((many,) + parts[0].shape, jnp.bfloat16),
                pltpu.SemaphoreType.DMA((many,)),
            ],
        ),
        compiler_params=pltpu.CompilerParams(vmem_limit_bytes=56 << 20),
        cost_estimate=pl.CostEstimate(flops=600000000, bytes_accessed=5000000, transcendentals=0),
        name="proj",
    )(owners, att, *parts, img_state, mod)


def mlp_kernel(many, *refs):
    pieces, w_ref = refs[:many], refs[many]
    *outs, up_s, down_s, hid_s, sem = refs[many + 1 :]
    shards, units, depth = up_s.shape
    group = 8
    chunks = shards // group
    chunk = group * units
    rows = pieces[0].shape[0]

    def load(half, dst, c):
        span = pl.ds(c * group, group)
        return pltpu.make_async_copy(w_ref.at[span, half], dst.at[span], sem.at[half * chunks + c])

    for c in range(chunks):
        load(0, up_s, c).start()
    for c in range(chunks):
        load(1, down_s, c).start()
    x = jnp.concatenate([piece[...] for piece in pieces], axis=0) if many > 1 else pieces[0][...]
    for c in range(chunks):
        load(0, up_s, c).wait()
        up = up_s[c * group : (c + 1) * group].reshape(chunk, depth)
        hid_s[:, c * chunk : (c + 1) * chunk] = jax.nn.gelu(dot(x, up, NT), approximate=True).astype(jnp.bfloat16)
    for c in range(chunks):
        load(1, down_s, c).wait()
    wide = 512
    for n in range(depth // wide):
        down = down_s[:, :, n * wide : (n + 1) * wide].reshape(chunks * chunk, wide)
        total = dot(hid_s[...], down, NN)
        for i, out in enumerate(outs):
            out[:, n * wide : (n + 1) * wide] = total[i * rows : (i + 1) * rows].astype(out.dtype)


def mlp(pieces, types, weights):
    shards, _, units, width = weights.shape
    rows = pieces[0].shape[0]
    many = len(pieces)
    return pl.pallas_call(
        functools.partial(mlp_kernel, many),
        out_shape=[jax.ShapeDtypeStruct((rows, width), t) for t in types],
        grid=(1,),
        in_specs=[pl.BlockSpec((rows, width), lambda i: (0, 0)) for _ in pieces]
        + [pl.BlockSpec(memory_space=pltpu.HBM)],
        out_specs=[pl.BlockSpec((rows, width), lambda i: (0, 0))] * len(types),
        scratch_shapes=[
            pltpu.VMEM((shards, units, width), jnp.bfloat16),
            pltpu.VMEM((shards, units, width), jnp.bfloat16),
            pltpu.VMEM((rows * many, shards * units), jnp.bfloat16),
            pltpu.SemaphoreType.DMA((shards // 4,)),
        ],
        compiler_params=pltpu.CompilerParams(vmem_limit_bytes=56 << 20),
        cost_estimate=pl.CostEstimate(
            flops=4 * rows * many * shards * units * width,
            bytes_accessed=4 * shards * units * width,
            transcendentals=0,
        ),
        name="mlp",
    )(*pieces, weights)


def finish_kernel(prompts, mod_ref, w_ref, *refs):
    *lists, mine_ref, others_ref = refs
    half = mine_ref.shape[1]
    each = len(lists) // prompts
    for p in range(prompts):
        resid, *terms = lists[p * each : (p + 1) * each]
        total = terms[0][...].astype(jnp.float32)
        for term in terms[1:]:
            total = total + term[...].astype(jnp.float32)
        two = resid[...].astype(jnp.float32) + mod_ref[p, 5:6, :] * total
        last = layer_norm(two) * (1.0 + mod_ref[p, 9:10, :]) + mod_ref[p, 8:9, :]
        vel = dot(w_ref[...], last.astype(jnp.bfloat16), (((0,), (1,)), ((), ())))
        mine_ref[p] = vel[0:half]
        others_ref[p] = vel[half:].astype(jnp.bfloat16)


def finish(lists, mod, w_last):
    prompts = len(lists)
    half = w_last.shape[1] // 2
    shape = (prompts, half, lists[0][0].shape[0])
    return pl.pallas_call(
        functools.partial(finish_kernel, prompts),
        out_shape=[jax.ShapeDtypeStruct(shape, jnp.float32), jax.ShapeDtypeStruct(shape, jnp.bfloat16)],
        compiler_params=pltpu.CompilerParams(vmem_limit_bytes=32 << 20),
        name="finish",
    )(mod, w_last, *[value for one in lists for value in one])


def shifted(value, axis, by):
    size = lax.axis_size(axis)
    return lax.ppermute(value, axis, [(i, (i + by) % size) for i in range(size)])


def swap(value, axis):
    return shifted(value, axis, 1)


def along_z(value, by):
    place = lambda z: z % 2 * 2 + z // 2
    pairs = [(place(z), place((z + by) % 4)) for z in range(4)]
    return lax.ppermute(value, ("cfg", "zhi"), pairs)


def local(
    img_state,
    txt_state,
    cond_vec,
    text_len,
    latent,
    w_mod,
    w_qkv_img,
    w_qkv_txt,
    w_attn_out,
    w_up,
    w_down,
    w_final,
):
    prompts = img_state.shape[1]
    rows = img_state.shape[2]
    width = img_state.shape[3]
    txt_rows = txt_state.shape[2]
    high = lax.axis_size("y")
    seqs = high * lax.axis_size("core")
    reqs = lax.axis_size("zhi") * lax.axis_size("x")
    everyone = reqs * seqs

    padding = jnp.zeros((prompts, TXT_PAD - txt_rows, width), jnp.bfloat16)
    mine = jnp.concatenate([img_state[0], txt_state[0], padding], axis=1)
    below = shifted(mine, "y", 1)
    above = shifted(mine, "y", -1)
    far = [shifted(below[p], "y", 1) if p % 2 == 0 else shifted(above[p], "y", -1) for p in range(prompts)]
    pairs = [mine, below, above]
    mates = [swap(block, "core") for block in pairs]
    tokens = [pairs + [far[p]] + mates + [swap(far[p], "core")] for p in range(prompts)]

    weights = lax.all_gather(
        jnp.stack([w_up, w_down])[None], ("x",) + SEQ, axis=0, tiled=True
    )

    cond_act = jax.nn.silu(cond_vec[0]).astype(jnp.bfloat16)
    part = dot(cond_act, w_mod, NT)
    cols = part.shape[1]
    lanes = -(-cols // 128) * 128
    part = jnp.pad(part, ((0, 0), (0, lanes - cols)))
    part = part.reshape(reqs, 1, prompts * lanes // 128, 128)
    part = jnp.broadcast_to(part, (reqs, seqs) + part.shape[2:]).reshape((everyone,) + part.shape[2:])
    got = lax.all_to_all(part, REQ + SEQ, 0, 0, tiled=True)
    got = got.reshape(everyone, prompts, lanes)[:, :, :cols]
    mod = jnp.swapaxes(got, 0, 1).reshape(prompts, 10, width)

    here, core = lax.axis_index("y"), lax.axis_index("core")
    level = (here + jnp.array([0, high - 1, 1, 2], jnp.int32)) % high
    owners = jnp.concatenate([2 * level + core, 2 * level + 1 - core]).astype(jnp.int32)
    inside = jnp.arange(TXT_PAD)
    index = owners[:, None] * txt_rows + inside[None, :]
    live = (inside < txt_rows)[None, None, :] & (index[None] < text_len[0][:, None, None])
    bias = jnp.where(live, 0.0, -1e30).astype(jnp.float32).reshape(prompts, seqs * TXT_PAD, 1)

    att = [
        attention(p, owners, tokens[p], mod, bias, w_qkv_img, w_qkv_txt) for p in range(prompts)
    ]
    late, _ = lax.optimization_barrier((w_attn_out, far[-1]))
    parts = [late] + [shifted(late, "y", by) for by in (1, -1, 2)]
    last = att[-1]
    att = [lax.all_to_all(a, SEQ, 0, 0, tiled=True) for a in att]
    att[0], parts, _ = lax.optimization_barrier((att[0], parts, last))
    parts = parts + [swap(part, "core") for part in parts]
    resid, normed = zip(
        *[project(p, owners, att[p], parts, img_state, mod) for p in range(prompts)]
    )
    f32, bf16 = jnp.float32, jnp.bfloat16
    own = mlp(list(normed), [f32, f32], weights)
    before = own[0]
    lists = []
    for p in range(prompts):
        on = 1 if p % 2 == 0 else -1
        first, second = along_z(normed[p], on), along_z(normed[p], -on)
        third = along_z(first, on)
        third, before = lax.optimization_barrier((third, before))
        (hop,) = mlp([third], [bf16], weights)
        first, second, before = lax.optimization_barrier((first, second, hop))
        direct, through = mlp([first, second], [bf16, f32], weights)
        through = (through + along_z(hop, on).astype(f32)).astype(bf16)
        before = through
        lists.append([resid[p], own[p], along_z(direct, -on), along_z(through, on)])

    half = latent.shape[2]
    branch = lax.axis_index("cfg")
    first = branch == 0
    w_last = jnp.where(first, w_final, jnp.concatenate([w_final[:, half:], w_final[:, :half]], axis=1))
    mine, others = finish(lists, mod, w_last)
    partner = swap(others, "cfg").astype(jnp.float32)
    cond_vel = jnp.where(first, mine, partner)
    uncond_vel = jnp.where(first, partner, mine)
    velocity = uncond_vel + 4.5 * (cond_vel - uncond_vel)
    latent_next = jnp.swapaxes(latent, 1, 2) - 0.04 * velocity
    return jnp.swapaxes(velocity, 1, 2), jnp.swapaxes(latent_next, 1, 2)


def solution(mesh):
    fine = Mesh(np.asarray(mesh.devices).reshape(2, 2, 4, 4, 2), ("cfg", "zhi", "x", "y", "core"))
    every = ("cfg",) + REQ + SEQ
    placed = (
        P("cfg", REQ, SEQ, None),
        P("cfg", REQ, SEQ, None),
        P("cfg", None, None),
        P("cfg", REQ),
        P(REQ, SEQ, "cfg"),
        P(REQ + SEQ, None),
        P(None, SEQ, None),
        P(None, SEQ, None),
        P(SEQ, None),
        P(every, None),
        P(every, None),
        P(),
    )
    return jax.shard_map(
        local,
        mesh=fine,
        in_specs=placed,
        out_specs=(P(REQ, SEQ, "cfg"), P(REQ, SEQ, "cfg")),
        check_vma=False,
    )
```

```python
import functools
import math

import jax
import jax.numpy as jnp
import numpy as np
from jax import lax
from jax.experimental import pallas as pl
from jax.experimental.pallas import tpu as pltpu
from jax.sharding import Mesh
from jax.sharding import PartitionSpec as P

HEAD = 64
SEQ = ("y", "core")
REQ = ("zhi", "x")
NT = (((1,), (1,)), ((), ()))
NN = (((1,), (0,)), ((), ()))
TN = (((0,), (0,)), ((), ()))
TXT_PAD = 32


def dot(a, b, dims):
    return lax.dot_general(a, b, dims, preferred_element_type=jnp.float32)


def layer_norm(value):
    mean = jnp.mean(value, axis=-1, keepdims=True)
    centered = value - mean
    spread = jnp.mean(centered * centered, axis=-1, keepdims=True)
    return centered * lax.rsqrt(spread + 1e-06)


def attn_kernel(prompt, many, idx_ref, *refs):
    pieces = refs[:many]
    mod_ref, bias_ref, wi_ref, wt_ref, out_ref, x_s, wi_s, wt_s, ai, at, k_s, v_s, q_s, x_sem, w_sem = refs[many:]
    block = x_s.shape[1]
    rows = block - TXT_PAD
    img = many * rows
    keys = many * block
    width = wt_s.shape[0] // 2
    heads = width // HEAD

    def take(s):
        piece = pieces[s] if len(pieces[s].shape) == 2 else pieces[s].at[prompt]
        return pltpu.make_async_copy(piece, x_s.at[s], x_sem.at[s])

    order = [(wi_ref, 0, wi_s, 0), (wi_ref, 2, wi_s, 1), (wi_ref, 1, wi_s, 2), (wt_ref, 2, wt_s, 0), (wt_ref, 1, wt_s, 1)]
    loads = [take(s) for s in range(many)] + [
        pltpu.make_async_copy(src.at[j], dst.at[pl.ds(i * width, width)], w_sem.at[n])
        for n, (src, j, dst, i) in enumerate(order)
    ]
    ahead = 3
    for load in loads[:ahead]:
        load.start()

    def modulated(part, scale, shift):
        normed = layer_norm(part.astype(jnp.float32))
        return (normed * (1.0 + mod_ref[0, scale : scale + 1, :]) + mod_ref[0, shift : shift + 1, :]).astype(
            jnp.bfloat16
        )

    def one_piece(s, carry):
        for n in range(many):

            @pl.when(s == n)
            def _(n=n):
                loads[n].wait()
                loads[n + ahead].start()

        ai[pl.ds(pl.multiple_of(s * rows, rows), rows), :] = modulated(x_s[s, 0:rows, :], 1, 0)
        at[pl.ds(pl.multiple_of(s * TXT_PAD, TXT_PAD), TXT_PAD), :] = modulated(x_s[s, rows:block, :], 7, 6)
        return carry

    lax.fori_loop(0, many, one_piece, 0)
    for load in loads[many + ahead :]:
        load.start()
    for load in loads[many:]:
        load.wait()
    ones = jnp.ones((16, keys), jnp.bfloat16)
    for h in range(heads):
        v_s[h, HEAD : HEAD + 16, :] = ones
        if h:
            q_s[h, 0 : h * HEAD, :] = jnp.zeros((h * HEAD, img), jnp.bfloat16)
        if h + 1 < heads:
            q_s[h, (h + 1) * HEAD :, :] = jnp.zeros((width - (h + 1) * HEAD, img), jnp.bfloat16)
    wide = 2 * rows

    def some_rows(c, carry):
        span = pl.ds(pl.multiple_of(c * wide, wide), wide)
        a = ai[span, :]
        k_s[span, :] = dot(a, wi_s[2 * width : 3 * width, :], NT).astype(jnp.bfloat16)
        both = dot(wi_s[0 : 2 * width, :], a, NT)
        query = (both[0:width] * (HEAD ** (-0.5) * math.log2(math.e))).astype(jnp.bfloat16)
        for h in range(heads):
            q_s[h, h * HEAD : (h + 1) * HEAD, span] = query[h * HEAD : (h + 1) * HEAD]
            v_s[h, 0:HEAD, span] = both[width + h * HEAD : width + (h + 1) * HEAD].astype(jnp.bfloat16)
        return carry

    lax.fori_loop(0, img // wide, some_rows, 0)
    a_txt = at[...]
    k_s[img:keys, :] = dot(a_txt, wt_s[width : 2 * width, :], NT).astype(jnp.bfloat16)
    v_txt = dot(wt_s[0:width, :], a_txt, NT).astype(jnp.bfloat16)
    for h in range(heads):
        v_s[h, 0:HEAD, img:keys] = v_txt[h * HEAD : (h + 1) * HEAD, :]

    def one_head(h, carry):
        query = q_s[h]
        s_img = dot(k_s[0:img, :], query, NN)
        s_txt = dot(k_s[img:keys, :], query, NN) + bias_ref[0]
        top = jnp.maximum(jnp.max(s_img, axis=0, keepdims=True), jnp.max(s_txt, axis=0, keepdims=True))
        p_img = jnp.exp2(s_img - top).astype(jnp.bfloat16)
        p_txt = jnp.exp2(s_txt - top).astype(jnp.bfloat16)
        o = dot(v_s[h, :, 0:img], p_img, NN) + dot(v_s[h, :, img:keys], p_txt, NN)
        o = (o[0:HEAD] / o[HEAD : HEAD + 1]).astype(jnp.bfloat16)
        for i in range(many):
            out_ref[idx_ref[i], pl.ds(pl.multiple_of(h * HEAD, HEAD), HEAD), :] = o[:, i * rows : (i + 1) * rows]
        return carry

    lax.fori_loop(0, heads, one_head, 0)


def attention(prompt, owners, pieces, mod, bias, w_img, w_txt):
    many = len(pieces)
    block, depth = pieces[0].shape[-2:]
    rows = block - TXT_PAD
    width = w_img.shape[1]
    heads = width // HEAD
    keys = many * block
    once = lambda *zeros: (lambda i, owners: zeros)
    stays = pl.BlockSpec(memory_space=pltpu.HBM)
    bf16 = jnp.bfloat16
    return pl.pallas_call(
        functools.partial(attn_kernel, prompt, many),
        out_shape=jax.ShapeDtypeStruct((many, width, rows), bf16),
        grid_spec=pltpu.PrefetchScalarGridSpec(
            num_scalar_prefetch=1,
            grid=(1,),
            in_specs=[stays] * many
            + [
                pl.BlockSpec((1, 10, depth), once(prompt, 0, 0)),
                pl.BlockSpec((1, many * TXT_PAD, 1), once(prompt, 0, 0)),
                stays,
                stays,
            ],
            out_specs=pl.BlockSpec((many, width, rows), once(0, 0, 0)),
            scratch_shapes=[
                pltpu.VMEM((many, block, depth), bf16),
                pltpu.VMEM((3 * width, depth), bf16),
                pltpu.VMEM((2 * width, depth), bf16),
                pltpu.VMEM((many * rows, depth), bf16),
                pltpu.VMEM((many * TXT_PAD, depth), bf16),
                pltpu.VMEM((keys, width), bf16),
                pltpu.VMEM((heads, HEAD + 16, keys), bf16),
                pltpu.VMEM((heads, width, many * rows), bf16),
                pltpu.SemaphoreType.DMA((many,)),
                pltpu.SemaphoreType.DMA((5,)),
            ],
        ),
        compiler_params=pltpu.CompilerParams(vmem_limit_bytes=56 << 20),
        cost_estimate=pl.CostEstimate(flops=8000000000, bytes_accessed=8000000, transcendentals=0),
        name="attn",
    )(owners, *pieces, mod, bias, w_img, w_txt)


def proj_kernel(many, prompts, idx_ref, *refs):
    atts, parts = refs[:prompts], refs[prompts : prompts + many]
    img_ref, mod_ref, resid_ref, normed_ref, w_s, att_s, sem = refs[prompts + many :]
    rows = img_ref.shape[2]
    loads, owner, at = [], [], 0
    size = parts[0].shape[0]
    for n, part in enumerate(parts):
        loads.append(pltpu.make_async_copy(part, w_s.at[pl.ds(at, part.shape[0])], sem.at[n]))
        at += part.shape[0]
    for load in loads:
        load.start()
    for p, att in enumerate(atts):
        for s in range(w_s.shape[0] // size):
            att_s[s * size : (s + 1) * size, p * rows : (p + 1) * rows] = att[idx_ref[s]]
    for load in loads:
        load.wait()
    total = dot(att_s[...], w_s[...], TN)
    for p in range(prompts):
        span = slice(p * rows, (p + 1) * rows)
        one = (img_ref[0, p].astype(jnp.float32) + mod_ref[p, 2:3, :] * total[span]).astype(jnp.bfloat16)
        resid_ref[span, :] = one
        normed = layer_norm(one.astype(jnp.float32)) * (1.0 + mod_ref[p, 4:5, :]) + mod_ref[p, 3:4, :]
        normed_ref[span, :] = normed.astype(jnp.bfloat16)


def project(owners, atts, parts, img_state, mod):
    prompts, rows, depth = img_state.shape[1:]
    many = len(parts)
    total = sum(part.shape[0] for part in parts)
    once = lambda *zeros: (lambda i, owners: zeros)
    return pl.pallas_call(
        functools.partial(proj_kernel, many, prompts),
        out_shape=[jax.ShapeDtypeStruct((prompts * rows, depth), jnp.bfloat16)] * 2,
        grid_spec=pltpu.PrefetchScalarGridSpec(
            num_scalar_prefetch=1,
            grid=(1,),
            in_specs=[pl.BlockSpec(att.shape, once(0, 0, 0)) for att in atts]
            + [pl.BlockSpec(memory_space=pltpu.HBM)] * many
            + [
                pl.BlockSpec((1, prompts, rows, depth), once(0, 0, 0, 0)),
                pl.BlockSpec((prompts, 10, depth), once(0, 0, 0)),
            ],
            out_specs=[pl.BlockSpec((prompts * rows, depth), once(0, 0))] * 2,
            scratch_shapes=[
                pltpu.VMEM((total, depth), jnp.bfloat16),
                pltpu.VMEM((total, prompts * rows), jnp.bfloat16),
                pltpu.SemaphoreType.DMA((many,)),
            ],
        ),
        compiler_params=pltpu.CompilerParams(vmem_limit_bytes=56 << 20),
        cost_estimate=pl.CostEstimate(flops=1200000000, bytes_accessed=5000000, transcendentals=0),
        name="proj",
    )(owners, *atts, *parts, img_state, mod)


def mlp_kernel(many, *refs):
    pieces, w_ref = refs[:many], refs[many]
    *outs, x_s, up_s, down_s, hid_s, sem = refs[many + 1 :]
    shards, units, depth = up_s.shape
    group = 8
    chunks = shards // group
    chunk = group * units

    def load(half, dst, c):
        span = pl.ds(c * group, group)
        return pltpu.make_async_copy(w_ref.at[span, half], dst.at[span], sem.at[half * chunks + c])

    load(0, up_s, 0).start()
    load(0, up_s, 1).start()
    at = 0
    for piece in pieces:
        x_s[at : at + piece.shape[0], :] = piece[...]
        at += piece.shape[0]

    def one_chunk(c, carry):
        load(0, up_s, c).wait()

        @pl.when(c + 2 < chunks)
        def _():
            load(0, up_s, c + 2).start()

        @pl.when(c + 2 >= chunks)
        def _():
            load(1, down_s, c + 2 - chunks).start()

        up = up_s[pl.ds(c * group, group)].reshape(chunk, depth)
        inner = jax.nn.gelu(dot(x_s[...], up, NT), approximate=True)
        hid_s[:, pl.ds(pl.multiple_of(c * chunk, chunk), chunk)] = inner.astype(jnp.bfloat16)
        return carry

    lax.fori_loop(0, chunks, one_chunk, 0)
    for c in range(2, chunks):
        load(1, down_s, c).start()
    for c in range(chunks):
        load(1, down_s, c).wait()
    wide = 512
    rows = outs[0].shape[0]

    def some_columns(n, carry):
        span = pl.ds(pl.multiple_of(n * wide, wide), wide)
        down = down_s[:, :, span].reshape(chunks * chunk, wide)
        total = dot(hid_s[...], down, NN)
        for i, out in enumerate(outs):
            out[:, span] = total[i * rows : (i + 1) * rows].astype(out.dtype)
        return carry

    lax.fori_loop(0, depth // wide, some_columns, 0)


def mlp(pieces, types, weights):
    shards, _, units, width = weights.shape
    many = len(pieces)
    count = sum(piece.shape[0] for piece in pieces)
    rows = count // len(types)
    return pl.pallas_call(
        functools.partial(mlp_kernel, many),
        out_shape=[jax.ShapeDtypeStruct((rows, width), t) for t in types],
        grid=(1,),
        in_specs=[pl.BlockSpec(piece.shape, lambda i: (0, 0)) for piece in pieces]
        + [pl.BlockSpec(memory_space=pltpu.HBM)],
        out_specs=[pl.BlockSpec((rows, width), lambda i: (0, 0))] * len(types),
        scratch_shapes=[
            pltpu.VMEM((count, width), jnp.bfloat16),
            pltpu.VMEM((shards, units, width), jnp.bfloat16),
            pltpu.VMEM((shards, units, width), jnp.bfloat16),
            pltpu.VMEM((count, shards * units), jnp.bfloat16),
            pltpu.SemaphoreType.DMA((shards // 4,)),
        ],
        compiler_params=pltpu.CompilerParams(vmem_limit_bytes=56 << 20),
        cost_estimate=pl.CostEstimate(
            flops=4 * count * shards * units * width,
            bytes_accessed=4 * shards * units * width,
            transcendentals=0,
        ),
        name="mlp",
    )(*pieces, weights)


def finish_kernel(mod_ref, w_ref, resid_ref, own_ref, *refs):
    *terms, mine_ref, others_ref = refs
    prompts, half, rows = mine_ref.shape
    for p in range(prompts):
        span = slice(p * rows, (p + 1) * rows)
        total = own_ref[span, :]
        for term in terms[2 * p : 2 * p + 2]:
            total = total + term[...].astype(jnp.float32)
        two = resid_ref[span, :].astype(jnp.float32) + mod_ref[p, 5:6, :] * total
        last = layer_norm(two) * (1.0 + mod_ref[p, 9:10, :]) + mod_ref[p, 8:9, :]
        vel = dot(w_ref[...], last.astype(jnp.bfloat16), (((0,), (1,)), ((), ())))
        mine_ref[p] = vel[0:half]
        others_ref[p] = vel[half:].astype(jnp.bfloat16)


def finish(resid, own, terms, mod, w_last):
    prompts = mod.shape[0]
    half = w_last.shape[1] // 2
    shape = (prompts, half, resid.shape[0] // prompts)
    return pl.pallas_call(
        finish_kernel,
        out_shape=[jax.ShapeDtypeStruct(shape, jnp.float32), jax.ShapeDtypeStruct(shape, jnp.bfloat16)],
        compiler_params=pltpu.CompilerParams(vmem_limit_bytes=32 << 20),
        name="finish",
    )(mod, w_last, resid, own, *terms)


def shifted(value, axis, by):
    size = lax.axis_size(axis)
    return lax.ppermute(value, axis, [(i, (i + by) % size) for i in range(size)])


def swap(value, axis):
    return shifted(value, axis, 1)


def along_z(value, by):
    place = lambda z: z % 2 * 2 + z // 2
    pairs = [(place(z), place((z + by) % 4)) for z in range(4)]
    return lax.ppermute(value, ("cfg", "zhi"), pairs)


def local(
    img_state,
    txt_state,
    cond_vec,
    text_len,
    latent,
    w_mod,
    w_qkv_img,
    w_qkv_txt,
    w_attn_out,
    w_up,
    w_down,
    w_final,
):
    prompts = img_state.shape[1]
    rows = img_state.shape[2]
    width = img_state.shape[3]
    txt_rows = txt_state.shape[2]
    high = lax.axis_size("y")
    seqs = high * lax.axis_size("core")
    reqs = lax.axis_size("zhi") * lax.axis_size("x")
    everyone = reqs * seqs

    padding = jnp.zeros((TXT_PAD - txt_rows, width), jnp.bfloat16)
    tokens, before = [], None
    for p in range(prompts):
        mine = jnp.concatenate([img_state[0, p], txt_state[0, p], padding], axis=0)
        if before is not None:
            mine, *before = lax.optimization_barrier((mine, *before))
        below, above = shifted(mine, "y", 1), shifted(mine, "y", -1)
        before = [below, above]
        far = shifted(below, "y", 1) if p % 2 == 0 else shifted(above, "y", -1)
        same = [mine, below, above, far]
        tokens.append(same + [swap(block, "core") for block in same])

    weights = lax.all_gather(
        jnp.stack([w_up, w_down])[None], ("x",) + SEQ, axis=0, tiled=True
    )

    cond_act = jax.nn.silu(cond_vec[0]).astype(jnp.bfloat16)
    part = dot(cond_act, w_mod, NT)
    cols = part.shape[1]
    lanes = -(-cols // 128) * 128
    part = jnp.pad(part, ((0, 0), (0, lanes - cols)))
    part = part.reshape(reqs, 1, prompts * lanes // 128, 128)
    part = jnp.broadcast_to(part, (reqs, seqs) + part.shape[2:]).reshape((everyone,) + part.shape[2:])
    got = lax.all_to_all(part, REQ + SEQ, 0, 0, tiled=True)
    got = got.reshape(everyone, prompts, lanes)[:, :, :cols]
    mod = jnp.swapaxes(got, 0, 1).reshape(prompts, 10, width)

    here, core = lax.axis_index("y"), lax.axis_index("core")
    level = (here + jnp.array([0, high - 1, 1, 2], jnp.int32)) % high
    owners = jnp.concatenate([2 * level + core, 2 * level + 1 - core]).astype(jnp.int32)
    inside = jnp.arange(TXT_PAD)
    index = owners[:, None] * txt_rows + inside[None, :]
    live = (inside < txt_rows)[None, None, :] & (index[None] < text_len[0][:, None, None])
    bias = jnp.where(live, 0.0, -1e30).astype(jnp.float32).reshape(prompts, seqs * TXT_PAD, 1)

    att = [
        attention(p, owners, tokens[p], mod, bias, w_qkv_img, w_qkv_txt) for p in range(prompts)
    ]
    late, _ = lax.optimization_barrier((w_attn_out, far))
    below, above = shifted(late, "y", 1), shifted(late, "y", -1)
    last = att[-1]
    att = [lax.all_to_all(a, SEQ, 0, 0, tiled=True) for a in att]
    below, above, last = lax.optimization_barrier((below, above, last))
    cut = late.shape[0] // 2
    far = [shifted(below[:cut], "y", 1), shifted(above[cut:], "y", -1)]
    parts = [late, below, above] + far
    parts = parts + [swap(part, "core") for part in parts]
    resid, normed = project(owners, att, parts, img_state, mod)
    f32, bf16 = jnp.float32, jnp.bfloat16
    low, high_rows = along_z(normed, 1), along_z(normed, -1)
    away = [along_z(low[:rows], 1), along_z(high_rows[rows:], -1)]
    (own,) = mlp([normed], [f32], weights)
    low, high_rows, before = lax.optimization_barrier((low, high_rows, own))
    low0, low1, high0, high1 = mlp([low, high_rows], [bf16, f32, f32, bf16], weights)
    away, before = lax.optimization_barrier((away, low0))
    hop0, hop1 = mlp(away, [bf16, bf16], weights)
    hop0, hop1 = along_z(hop0, 1), along_z(hop1, -1)
    terms = [along_z(low0, -1), along_z((high0 + hop0.astype(f32)).astype(bf16), 1)]
    terms += [along_z(high1, 1), along_z((low1 + hop1.astype(f32)).astype(bf16), -1)]

    half = latent.shape[2]
    branch = lax.axis_index("cfg")
    first = branch == 0
    w_last = jnp.where(first, w_final, jnp.concatenate([w_final[:, half:], w_final[:, :half]], axis=1))
    mine, others = finish(resid, own, terms, mod, w_last)
    partner = swap(others, "cfg").astype(jnp.float32)
    cond_vel = jnp.where(first, mine, partner)
    uncond_vel = jnp.where(first, partner, mine)
    velocity = uncond_vel + 4.5 * (cond_vel - uncond_vel)
    latent_next = jnp.swapaxes(latent, 1, 2) - 0.04 * velocity
    return jnp.swapaxes(velocity, 1, 2), jnp.swapaxes(latent_next, 1, 2)


def solution(mesh):
    fine = Mesh(np.asarray(mesh.devices).reshape(2, 2, 4, 4, 2), ("cfg", "zhi", "x", "y", "core"))
    every = ("cfg",) + REQ + SEQ
    placed = (
        P("cfg", REQ, SEQ, None),
        P("cfg", REQ, SEQ, None),
        P("cfg", None, None),
        P("cfg", REQ),
        P(REQ, SEQ, "cfg"),
        P(REQ + SEQ, None),
        P(None, SEQ, None),
        P(None, SEQ, None),
        P(SEQ, None),
        P(every, None),
        P(every, None),
        P(),
    )
    return jax.shard_map(
        local,
        mesh=fine,
        in_specs=placed,
        out_specs=(P(REQ, SEQ, "cfg"), P(REQ, SEQ, "cfg")),
        check_vma=False,
    )
```

```python
import functools
import math

import jax
import jax.numpy as jnp
import numpy as np
from jax import lax
from jax.experimental import pallas as pl
from jax.experimental.pallas import tpu as pltpu
from jax.sharding import Mesh
from jax.sharding import PartitionSpec as P

HEAD = 64
SEQ = ("y", "core")
REQ = ("zhi", "x")
NT = (((1,), (1,)), ((), ()))
NN = (((1,), (0,)), ((), ()))
TN = (((0,), (0,)), ((), ()))
TXT_PAD = 32


def dot(a, b, dims):
    return lax.dot_general(a, b, dims, preferred_element_type=jnp.float32)


def layer_norm(value):
    mean = jnp.mean(value, axis=-1, keepdims=True)
    centered = value - mean
    spread = jnp.mean(centered * centered, axis=-1, keepdims=True)
    return centered * lax.rsqrt(spread + 1e-06)


def attn_kernel(prompt, many, idx_ref, *refs):
    pieces = refs[:many]
    mod_ref, bias_ref, wi_ref, wt_ref, out_ref, x_s, wi_s, wt_s, ai, at, k_s, v_s, q_s, x_sem, w_sem = refs[many:]
    block = x_s.shape[1]
    rows = block - TXT_PAD
    img = many * rows
    keys = many * block
    width = wt_s.shape[0] // 2
    heads = width // HEAD

    def take(s):
        piece = pieces[s] if len(pieces[s].shape) == 2 else pieces[s].at[prompt]
        return pltpu.make_async_copy(piece, x_s.at[s], x_sem.at[s])

    order = [(wi_ref, 0, wi_s, 0), (wi_ref, 2, wi_s, 1), (wi_ref, 1, wi_s, 2), (wt_ref, 2, wt_s, 0), (wt_ref, 1, wt_s, 1)]
    loads = [take(s) for s in range(many)] + [
        pltpu.make_async_copy(src.at[j], dst.at[pl.ds(i * width, width)], w_sem.at[n])
        for n, (src, j, dst, i) in enumerate(order)
    ]
    ahead = 3
    for load in loads[:ahead]:
        load.start()

    def modulated(part, scale, shift):
        normed = layer_norm(part.astype(jnp.float32))
        return (normed * (1.0 + mod_ref[0, scale : scale + 1, :]) + mod_ref[0, shift : shift + 1, :]).astype(
            jnp.bfloat16
        )

    for s in range(many):
        loads[s].wait()
        loads[s + ahead].start()
        ai[s * rows : (s + 1) * rows, :] = modulated(x_s[s, 0:rows, :], 1, 0)
        at[s * TXT_PAD : (s + 1) * TXT_PAD, :] = modulated(x_s[s, rows:block, :], 7, 6)
    for load in loads[many + ahead :]:
        load.start()
    for load in loads[many:]:
        load.wait()
    ones = jnp.ones((16, keys), jnp.bfloat16)
    for h in range(heads):
        v_s[h, HEAD : HEAD + 16, :] = ones
        if h:
            q_s[h, 0 : h * HEAD, :] = jnp.zeros((h * HEAD, img), jnp.bfloat16)
        if h + 1 < heads:
            q_s[h, (h + 1) * HEAD :, :] = jnp.zeros((width - (h + 1) * HEAD, img), jnp.bfloat16)
    wide = 4 * rows

    def some_rows(c, carry):
        span = pl.ds(pl.multiple_of(c * wide, wide), wide)
        a = ai[span, :]
        k_s[span, :] = dot(a, wi_s[2 * width : 3 * width, :], NT).astype(jnp.bfloat16)
        both = dot(wi_s[0 : 2 * width, :], a, NT)
        query = (both[0:width] * (HEAD ** (-0.5) * math.log2(math.e))).astype(jnp.bfloat16)
        for h in range(heads):
            q_s[h, h * HEAD : (h + 1) * HEAD, span] = query[h * HEAD : (h + 1) * HEAD]
            v_s[h, 0:HEAD, span] = both[width + h * HEAD : width + (h + 1) * HEAD].astype(jnp.bfloat16)
        return carry

    lax.fori_loop(0, img // wide, some_rows, 0)
    a_txt = at[...]
    k_s[img:keys, :] = dot(a_txt, wt_s[width : 2 * width, :], NT).astype(jnp.bfloat16)
    v_txt = dot(wt_s[0:width, :], a_txt, NT).astype(jnp.bfloat16)
    for h in range(heads):
        v_s[h, 0:HEAD, img:keys] = v_txt[h * HEAD : (h + 1) * HEAD, :]

    def one_head(h, carry):
        query = q_s[h]
        s_img = dot(k_s[0:img, :], query, NN)
        s_txt = dot(k_s[img:keys, :], query, NN) + bias_ref[0]
        top = jnp.maximum(jnp.max(s_img, axis=0, keepdims=True), jnp.max(s_txt, axis=0, keepdims=True))
        p_img = jnp.exp2(s_img - top).astype(jnp.bfloat16)
        p_txt = jnp.exp2(s_txt - top).astype(jnp.bfloat16)
        o = dot(v_s[h, :, 0:img], p_img, NN) + dot(v_s[h, :, img:keys], p_txt, NN)
        o = (o[0:HEAD] / o[HEAD : HEAD + 1]).astype(jnp.bfloat16)
        for i in range(many):
            out_ref[idx_ref[i], pl.ds(pl.multiple_of(h * HEAD, HEAD), HEAD), :] = o[:, i * rows : (i + 1) * rows]
        return carry

    lax.fori_loop(0, heads, one_head, 0)


def attention(prompt, owners, pieces, mod, bias, w_img, w_txt):
    many = len(pieces)
    block, depth = pieces[0].shape[-2:]
    rows = block - TXT_PAD
    width = w_img.shape[1]
    heads = width // HEAD
    keys = many * block
    once = lambda *zeros: (lambda i, owners: zeros)
    stays = pl.BlockSpec(memory_space=pltpu.HBM)
    bf16 = jnp.bfloat16
    return pl.pallas_call(
        functools.partial(attn_kernel, prompt, many),
        out_shape=jax.ShapeDtypeStruct((many, width, rows), bf16),
        grid_spec=pltpu.PrefetchScalarGridSpec(
            num_scalar_prefetch=1,
            grid=(1,),
            in_specs=[stays] * many
            + [
                pl.BlockSpec((1, 10, depth), once(prompt, 0, 0)),
                pl.BlockSpec((1, many * TXT_PAD, 1), once(prompt, 0, 0)),
                stays,
                stays,
            ],
            out_specs=pl.BlockSpec((many, width, rows), once(0, 0, 0)),
            scratch_shapes=[
                pltpu.VMEM((many, block, depth), bf16),
                pltpu.VMEM((3 * width, depth), bf16),
                pltpu.VMEM((2 * width, depth), bf16),
                pltpu.VMEM((many * rows, depth), bf16),
                pltpu.VMEM((many * TXT_PAD, depth), bf16),
                pltpu.VMEM((keys, width), bf16),
                pltpu.VMEM((heads, HEAD + 16, keys), bf16),
                pltpu.VMEM((heads, width, many * rows), bf16),
                pltpu.SemaphoreType.DMA((many,)),
                pltpu.SemaphoreType.DMA((5,)),
            ],
        ),
        compiler_params=pltpu.CompilerParams(vmem_limit_bytes=56 << 20),
        cost_estimate=pl.CostEstimate(flops=8000000000, bytes_accessed=8000000, transcendentals=0),
        name="attn",
    )(owners, *pieces, mod, bias, w_img, w_txt)


def order_kernel(idx_ref, att_ref, out_ref):
    size = att_ref.shape[1]
    for s in range(att_ref.shape[0]):
        out_ref[s * size : (s + 1) * size, :] = att_ref[idx_ref[s]]


def ordered(owners, att):
    many, size, rows = att.shape
    return pl.pallas_call(
        order_kernel,
        out_shape=jax.ShapeDtypeStruct((many * size, rows), att.dtype),
        grid_spec=pltpu.PrefetchScalarGridSpec(
            num_scalar_prefetch=1,
            grid=(1,),
            in_specs=[pl.BlockSpec(att.shape, lambda i, owners: (0, 0, 0))],
            out_specs=pl.BlockSpec((many * size, rows), lambda i, owners: (0, 0)),
        ),
        cost_estimate=pl.CostEstimate(flops=4000000000, bytes_accessed=8000000, transcendentals=0),
        name="order",
    )(owners, att)


def proj_kernel(many, att_ref, *refs):
    parts = refs[:many]
    img_ref, mod_ref, resid_ref, normed_ref, w_s, sem = refs[many:]
    loads, at = [], 0
    for n, part in enumerate(parts):
        loads.append(pltpu.make_async_copy(part, w_s.at[pl.ds(at, part.shape[0])], sem.at[n]))
        at += part.shape[0]
    for load in loads:
        load.start()
    for load in loads:
        load.wait()
    total = dot(att_ref[...], w_s[...], TN)
    one = (img_ref[0, 0].astype(jnp.float32) + mod_ref[0, 2:3, :] * total).astype(jnp.bfloat16)
    resid_ref[...] = one
    normed = layer_norm(one.astype(jnp.float32)) * (1.0 + mod_ref[0, 4:5, :]) + mod_ref[0, 3:4, :]
    normed_ref[...] = normed.astype(jnp.bfloat16)


def project(prompt, att, parts, img_state, mod):
    rows, depth = img_state.shape[2:]
    many = len(parts)
    once = lambda *zeros: (lambda i: zeros)
    return pl.pallas_call(
        functools.partial(proj_kernel, many),
        out_shape=[jax.ShapeDtypeStruct((rows, depth), jnp.bfloat16)] * 2,
        grid=(1,),
        in_specs=[pl.BlockSpec(att.shape, once(0, 0))]
        + [pl.BlockSpec(memory_space=pltpu.HBM)] * many
        + [
            pl.BlockSpec((1, 1, rows, depth), once(0, prompt, 0, 0)),
            pl.BlockSpec((1, 10, depth), once(prompt, 0, 0)),
        ],
        out_specs=[pl.BlockSpec((rows, depth), once(0, 0))] * 2,
        scratch_shapes=[
            pltpu.VMEM((att.shape[0], depth), jnp.bfloat16),
            pltpu.SemaphoreType.DMA((many,)),
        ],
        compiler_params=pltpu.CompilerParams(vmem_limit_bytes=56 << 20),
        cost_estimate=pl.CostEstimate(flops=8000000000, bytes_accessed=5000000, transcendentals=0),
        name="proj",
    )(att, *parts, img_state, mod)


def mlp_kernel(*refs):
    *pieces, up_ref, down_ref, out_ref, x_s, acc = refs
    step = pl.program_id(0)

    @pl.when(step == 0)
    def _():
        at = 0
        for piece in pieces:
            x_s[at : at + piece.shape[0], :] = piece[...]
            at += piece.shape[0]

    depth = up_ref.shape[-1]
    up = up_ref[...].reshape(-1, depth)
    down = down_ref[...].reshape(-1, depth)
    hidden = jax.nn.gelu(dot(x_s[...], up, NT), approximate=True).astype(jnp.bfloat16)
    term = dot(hidden, down, NN)

    @pl.when(step == 0)
    def _():
        acc[...] = term

    @pl.when(step > 0)
    def _():
        acc[...] += term

    @pl.when(step == pl.num_programs(0) - 1)
    def _():
        out_ref[...] = acc[...].astype(out_ref.dtype)


def mlp(pieces, weights, out_type):
    shards, _, units, width = weights.shape
    many = 16
    count = sum(piece.shape[0] for piece in pieces)
    return pl.pallas_call(
        mlp_kernel,
        out_shape=jax.ShapeDtypeStruct((count, width), out_type),
        grid=(shards // many,),
        in_specs=[
            *[pl.BlockSpec(piece.shape, lambda i: (0, 0)) for piece in pieces],
            pl.BlockSpec((many, 1, units, width), lambda i: (i, 0, 0, 0)),
            pl.BlockSpec((many, 1, units, width), lambda i: (i, 1, 0, 0)),
        ],
        out_specs=pl.BlockSpec((count, width), lambda i: (0, 0)),
        scratch_shapes=[pltpu.VMEM((count, width), jnp.bfloat16), pltpu.VMEM((count, width), jnp.float32)],
        compiler_params=pltpu.CompilerParams(vmem_limit_bytes=56 << 20),
        cost_estimate=pl.CostEstimate(
            flops=4 * count * shards * units * width,
            bytes_accessed=4 * shards * units * width,
            transcendentals=0,
        ),
        name="mlp",
    )(*pieces, weights, weights)


def finish_kernel(mod_ref, w_ref, own_ref, back_ref, *refs):
    *resid, mine_ref, others_ref = refs
    prompts, half, rows = mine_ref.shape
    for p in range(prompts):
        span = slice(p * rows, (p + 1) * rows)
        total = own_ref[span, :] + back_ref[span, :].astype(jnp.float32)
        two = resid[p][...].astype(jnp.float32) + mod_ref[p, 5:6, :] * total
        last = layer_norm(two) * (1.0 + mod_ref[p, 9:10, :]) + mod_ref[p, 8:9, :]
        vel = dot(w_ref[...], last.astype(jnp.bfloat16), (((0,), (1,)), ((), ())))
        mine_ref[p] = vel[0:half]
        others_ref[p] = vel[half:].astype(jnp.bfloat16)


def finish(resid, own, back, mod, w_last):
    prompts = mod.shape[0]
    half = w_last.shape[1] // 2
    shape = (prompts, half, resid[0].shape[0])
    return pl.pallas_call(
        finish_kernel,
        out_shape=[jax.ShapeDtypeStruct(shape, jnp.float32), jax.ShapeDtypeStruct(shape, jnp.bfloat16)],
        compiler_params=pltpu.CompilerParams(vmem_limit_bytes=32 << 20),
        name="finish",
    )(mod, w_last, own, back, *resid)


def shifted(value, axis, by):
    size = lax.axis_size(axis)
    return lax.ppermute(value, axis, [(i, (i + by) % size) for i in range(size)])


def swap(value, axis):
    return shifted(value, axis, 1)


def local(
    img_state,
    txt_state,
    cond_vec,
    text_len,
    latent,
    w_mod,
    w_qkv_img,
    w_qkv_txt,
    w_attn_out,
    w_up,
    w_down,
    w_final,
):
    prompts = img_state.shape[1]
    rows = img_state.shape[2]
    width = img_state.shape[3]
    txt_rows = txt_state.shape[2]
    high = lax.axis_size("y")
    seqs = high * lax.axis_size("core")
    reqs = lax.axis_size("zhi") * lax.axis_size("x")
    everyone = reqs * seqs

    padding = jnp.zeros((prompts, TXT_PAD - txt_rows, width), jnp.bfloat16)
    mine = jnp.concatenate([img_state[0], txt_state[0], padding], axis=1)
    below, above = shifted(mine, "y", 1), shifted(mine, "y", -1)
    far = [shifted(below[p], "y", 1) if p % 2 == 0 else shifted(above[p], "y", -1) for p in range(prompts)]
    pairs = [mine, below, above]
    mates = [swap(block, "core") for block in pairs]
    tokens = [pairs + [far[p]] + mates + [swap(far[p], "core")] for p in range(prompts)]

    weights = lax.all_gather(jnp.stack([w_up, w_down])[None], REQ + SEQ, axis=0, tiled=True)

    cond_act = jax.nn.silu(cond_vec[0]).astype(jnp.bfloat16)
    part = dot(cond_act, w_mod, NT)
    cols = part.shape[1]
    lanes = -(-cols // 128) * 128
    part = jnp.pad(part, ((0, 0), (0, lanes - cols)))
    part = part.reshape(reqs, 1, prompts * lanes // 128, 128)
    part = jnp.broadcast_to(part, (reqs, seqs) + part.shape[2:]).reshape((everyone,) + part.shape[2:])
    got = lax.all_to_all(part, REQ + SEQ, 0, 0, tiled=True)
    got = got.reshape(everyone, prompts, lanes)[:, :, :cols]
    mod = jnp.swapaxes(got, 0, 1).reshape(prompts, 10, width)

    here, core = lax.axis_index("y"), lax.axis_index("core")
    level = (here + jnp.array([0, high - 1, 1, 2], jnp.int32)) % high
    owners = jnp.concatenate([2 * level + core, 2 * level + 1 - core]).astype(jnp.int32)
    inside = jnp.arange(TXT_PAD)
    index = owners[:, None] * txt_rows + inside[None, :]
    live = (inside < txt_rows)[None, None, :] & (index[None] < text_len[0][:, None, None])
    bias = jnp.where(live, 0.0, -1e30).astype(jnp.float32).reshape(prompts, seqs * TXT_PAD, 1)

    att = [
        attention(p, owners, tokens[p], mod, bias, w_qkv_img, w_qkv_txt) for p in range(prompts)
    ]
    late, _ = lax.optimization_barrier((w_attn_out, far[-1]))
    below, above = shifted(late, "y", 1), shifted(late, "y", -1)
    below, above, lead = lax.optimization_barrier((below, above, att[1]))
    cut = late.shape[0] // 2
    far = [shifted(below[:cut], "y", 1), shifted(above[cut:], "y", -1)]
    lead = lax.all_to_all(lead, SEQ, 0, 0, tiled=True)
    lead, far, below, above, last = lax.optimization_barrier((lead, far, below, above, att[0]))
    parts = [late, below, above] + list(far)
    parts = parts + [swap(part, "core") for part in parts]
    last = lax.all_to_all(last, SEQ, 0, 0, tiled=True)
    resid1, normed1 = project(1, ordered(owners, lead), parts, img_state, mod)
    other1 = swap(normed1, "cfg")
    last, other1 = lax.optimization_barrier((ordered(owners, last), other1))
    resid0, normed0 = project(0, last, parts, img_state, mod)
    other0 = swap(normed0, "cfg")
    back = swap(mlp([other0, other1], weights, jnp.bfloat16), "cfg")
    own = mlp([normed0, normed1], weights, jnp.float32)
    resid = [resid0, resid1]

    half = latent.shape[2]
    branch = lax.axis_index("cfg")
    first = branch == 0
    w_last = jnp.where(first, w_final, jnp.concatenate([w_final[:, half:], w_final[:, :half]], axis=1))
    mine, others = finish(resid, own, back, mod, w_last)
    partner = swap(others, "cfg").astype(jnp.float32)
    cond_vel = jnp.where(first, mine, partner)
    uncond_vel = jnp.where(first, partner, mine)
    velocity = uncond_vel + 4.5 * (cond_vel - uncond_vel)
    latent_next = jnp.swapaxes(latent, 1, 2) - 0.04 * velocity
    return jnp.swapaxes(velocity, 1, 2), jnp.swapaxes(latent_next, 1, 2)


def solution(mesh):
    fine = Mesh(np.asarray(mesh.devices).reshape(2, 2, 4, 4, 2), ("cfg", "zhi", "x", "y", "core"))
    every = ("cfg",) + REQ + SEQ
    placed = (
        P("cfg", REQ, SEQ, None),
        P("cfg", REQ, SEQ, None),
        P("cfg", None, None),
        P("cfg", REQ),
        P(REQ, SEQ, "cfg"),
        P(REQ + SEQ, None),
        P(None, SEQ, None),
        P(None, SEQ, None),
        P(SEQ, None),
        P(every, None),
        P(every, None),
        P(),
    )
    return jax.shard_map(
        local,
        mesh=fine,
        in_specs=placed,
        out_specs=(P(REQ, SEQ, "cfg"), P(REQ, SEQ, "cfg")),
        check_vma=False,
    )
```

```python
import functools
import math

import jax
import jax.numpy as jnp
import numpy as np
from jax import lax
from jax.experimental import pallas as pl
from jax.experimental.pallas import tpu as pltpu
from jax.sharding import Mesh
from jax.sharding import PartitionSpec as P

HEAD = 64
SEQ = ("y", "core")
REQ = ("zhi", "x")
NT = (((1,), (1,)), ((), ()))
NN = (((1,), (0,)), ((), ()))
TN = (((0,), (0,)), ((), ()))
TXT_PAD = 32


def dot(a, b, dims):
    return lax.dot_general(a, b, dims, preferred_element_type=jnp.float32)


def layer_norm(value):
    mean = jnp.mean(value, axis=-1, keepdims=True)
    centered = value - mean
    spread = jnp.mean(centered * centered, axis=-1, keepdims=True)
    return centered * lax.rsqrt(spread + 1e-06)


def attn_kernel(prompt, many, idx_ref, *refs):
    pieces = refs[:many]
    mod_ref, bias_ref, wi_ref, wt_ref, out_ref, x_s, wi_s, wt_s, ai, at, k_s, v_s, q_s, x_sem, w_sem = refs[many:]
    block = x_s.shape[1]
    rows = block - TXT_PAD
    img = many * rows
    keys = many * block
    width = wt_s.shape[0] // 2
    heads = width // HEAD

    def take(s):
        piece = pieces[s] if len(pieces[s].shape) == 2 else pieces[s].at[prompt]
        return pltpu.make_async_copy(piece, x_s.at[s], x_sem.at[s])

    order = [(wi_ref, 0, wi_s, 0), (wi_ref, 2, wi_s, 1), (wi_ref, 1, wi_s, 2), (wt_ref, 2, wt_s, 0), (wt_ref, 1, wt_s, 1)]
    loads = [take(s) for s in range(many)] + [
        pltpu.make_async_copy(src.at[j], dst.at[pl.ds(i * width, width)], w_sem.at[n])
        for n, (src, j, dst, i) in enumerate(order)
    ]
    ahead = 3
    for load in loads[:ahead]:
        load.start()

    def modulated(part, scale, shift):
        normed = layer_norm(part.astype(jnp.float32))
        return (normed * (1.0 + mod_ref[0, scale : scale + 1, :]) + mod_ref[0, shift : shift + 1, :]).astype(
            jnp.bfloat16
        )

    for s in range(many):
        loads[s].wait()
        loads[s + ahead].start()
        ai[s * rows : (s + 1) * rows, :] = modulated(x_s[s, 0:rows, :], 1, 0)
        at[s * TXT_PAD : (s + 1) * TXT_PAD, :] = modulated(x_s[s, rows:block, :], 7, 6)
    for load in loads[many + ahead :]:
        load.start()
    for load in loads[many:]:
        load.wait()
    ones = jnp.ones((16, keys), jnp.bfloat16)
    for h in range(heads):
        v_s[h, HEAD : HEAD + 16, :] = ones
        if h:
            q_s[h, 0 : h * HEAD, :] = jnp.zeros((h * HEAD, img), jnp.bfloat16)
        if h + 1 < heads:
            q_s[h, (h + 1) * HEAD :, :] = jnp.zeros((width - (h + 1) * HEAD, img), jnp.bfloat16)
    wide = 4 * rows

    def some_rows(c, carry):
        span = pl.ds(pl.multiple_of(c * wide, wide), wide)
        a = ai[span, :]
        k_s[span, :] = dot(a, wi_s[2 * width : 3 * width, :], NT).astype(jnp.bfloat16)
        both = dot(wi_s[0 : 2 * width, :], a, NT)
        query = (both[0:width] * (HEAD ** (-0.5) * math.log2(math.e))).astype(jnp.bfloat16)
        for h in range(heads):
            q_s[h, h * HEAD : (h + 1) * HEAD, span] = query[h * HEAD : (h + 1) * HEAD]
            v_s[h, 0:HEAD, span] = both[width + h * HEAD : width + (h + 1) * HEAD].astype(jnp.bfloat16)
        return carry

    lax.fori_loop(0, img // wide, some_rows, 0)
    a_txt = at[...]
    k_s[img:keys, :] = dot(a_txt, wt_s[width : 2 * width, :], NT).astype(jnp.bfloat16)
    v_txt = dot(wt_s[0:width, :], a_txt, NT).astype(jnp.bfloat16)
    for h in range(heads):
        v_s[h, 0:HEAD, img:keys] = v_txt[h * HEAD : (h + 1) * HEAD, :]

    def one_head(h, carry):
        query = q_s[h]
        s_img = dot(k_s[0:img, :], query, NN)
        s_txt = dot(k_s[img:keys, :], query, NN) + bias_ref[0]
        top = jnp.maximum(jnp.max(s_img, axis=0, keepdims=True), jnp.max(s_txt, axis=0, keepdims=True))
        p_img = jnp.exp2(s_img - top).astype(jnp.bfloat16)
        p_txt = jnp.exp2(s_txt - top).astype(jnp.bfloat16)
        o = dot(v_s[h, :, 0:img], p_img, NN) + dot(v_s[h, :, img:keys], p_txt, NN)
        o = (o[0:HEAD] / o[HEAD : HEAD + 1]).astype(jnp.bfloat16)
        for i in range(many):
            out_ref[idx_ref[i], pl.ds(pl.multiple_of(h * HEAD, HEAD), HEAD), :] = o[:, i * rows : (i + 1) * rows]
        return carry

    lax.fori_loop(0, heads, one_head, 0)


def attention(prompt, owners, pieces, mod, bias, w_img, w_txt):
    many = len(pieces)
    block, depth = pieces[0].shape[-2:]
    rows = block - TXT_PAD
    width = w_img.shape[1]
    heads = width // HEAD
    keys = many * block
    once = lambda *zeros: (lambda i, owners: zeros)
    stays = pl.BlockSpec(memory_space=pltpu.HBM)
    bf16 = jnp.bfloat16
    return pl.pallas_call(
        functools.partial(attn_kernel, prompt, many),
        out_shape=jax.ShapeDtypeStruct((many, width, rows), bf16),
        grid_spec=pltpu.PrefetchScalarGridSpec(
            num_scalar_prefetch=1,
            grid=(1,),
            in_specs=[stays] * many
            + [
                pl.BlockSpec((1, 10, depth), once(prompt, 0, 0)),
                pl.BlockSpec((1, many * TXT_PAD, 1), once(prompt, 0, 0)),
                stays,
                stays,
            ],
            out_specs=pl.BlockSpec((many, width, rows), once(0, 0, 0)),
            scratch_shapes=[
                pltpu.VMEM((many, block, depth), bf16),
                pltpu.VMEM((3 * width, depth), bf16),
                pltpu.VMEM((2 * width, depth), bf16),
                pltpu.VMEM((many * rows, depth), bf16),
                pltpu.VMEM((many * TXT_PAD, depth), bf16),
                pltpu.VMEM((keys, width), bf16),
                pltpu.VMEM((heads, HEAD + 16, keys), bf16),
                pltpu.VMEM((heads, width, many * rows), bf16),
                pltpu.SemaphoreType.DMA((many,)),
                pltpu.SemaphoreType.DMA((5,)),
            ],
        ),
        compiler_params=pltpu.CompilerParams(vmem_limit_bytes=56 << 20),
        cost_estimate=pl.CostEstimate(flops=8000000000, bytes_accessed=8000000, transcendentals=0),
        name="attn",
    )(owners, *pieces, mod, bias, w_img, w_txt)


def pass_on(value):
    anywhere = pl.BlockSpec(memory_space=pl.ANY)
    return pl.pallas_call(
        lambda value_ref, out_ref: None,
        out_shape=jax.ShapeDtypeStruct(value.shape, value.dtype),
        in_specs=[anywhere],
        out_specs=anywhere,
        input_output_aliases={0: 0},
        cost_estimate=pl.CostEstimate(flops=4000000000, bytes_accessed=8000000, transcendentals=0),
        name="pass_on",
    )(value)


def proj_kernel(many, idx_ref, att_ref, *refs):
    parts = refs[:many]
    img_ref, mod_ref, resid_ref, normed_ref, w_s, att_s, sem = refs[many:]
    size = att_ref.shape[1]
    loads, at = [], 0
    for n, part in enumerate(parts):
        loads.append(pltpu.make_async_copy(part, w_s.at[pl.ds(at, part.shape[0])], sem.at[n]))
        at += part.shape[0]
    for load in loads:
        load.start()
    for s in range(att_ref.shape[0]):
        att_s[s * size : (s + 1) * size, :] = att_ref[idx_ref[s]]
    for load in loads:
        load.wait()
    total = dot(att_s[...], w_s[...], TN)
    one = (img_ref[0, 0].astype(jnp.float32) + mod_ref[0, 2:3, :] * total).astype(jnp.bfloat16)
    resid_ref[...] = one
    normed = layer_norm(one.astype(jnp.float32)) * (1.0 + mod_ref[0, 4:5, :]) + mod_ref[0, 3:4, :]
    normed_ref[...] = normed.astype(jnp.bfloat16)


def project(prompt, owners, att, parts, img_state, mod):
    rows, depth = img_state.shape[2:]
    many = len(parts)
    total = att.shape[0] * att.shape[1]
    once = lambda *zeros: (lambda i, owners: zeros)
    return pl.pallas_call(
        functools.partial(proj_kernel, many),
        out_shape=[jax.ShapeDtypeStruct((rows, depth), jnp.bfloat16)] * 2,
        grid_spec=pltpu.PrefetchScalarGridSpec(
            num_scalar_prefetch=1,
            grid=(1,),
            in_specs=[pl.BlockSpec(att.shape, once(0, 0, 0))]
            + [pl.BlockSpec(memory_space=pltpu.HBM)] * many
            + [
                pl.BlockSpec((1, 1, rows, depth), once(0, prompt, 0, 0)),
                pl.BlockSpec((1, 10, depth), once(prompt, 0, 0)),
            ],
            out_specs=[pl.BlockSpec((rows, depth), once(0, 0))] * 2,
            scratch_shapes=[
                pltpu.VMEM((total, depth), jnp.bfloat16),
                pltpu.VMEM((total, rows), jnp.bfloat16),
                pltpu.SemaphoreType.DMA((many,)),
            ],
        ),
        compiler_params=pltpu.CompilerParams(vmem_limit_bytes=56 << 20),
        cost_estimate=pl.CostEstimate(flops=8000000000, bytes_accessed=5000000, transcendentals=0),
        name="proj",
    )(owners, att, *parts, img_state, mod)


def mlp_kernel(*refs):
    *pieces, up_ref, down_ref, out_ref, x_s, acc = refs
    step = pl.program_id(0)

    @pl.when(step == 0)
    def _():
        at = 0
        for piece in pieces:
            x_s[at : at + piece.shape[0], :] = piece[...]
            at += piece.shape[0]

    depth = up_ref.shape[-1]
    up = up_ref[...].reshape(-1, depth)
    down = down_ref[...].reshape(-1, depth)
    hidden = jax.nn.gelu(dot(x_s[...], up, NT), approximate=True).astype(jnp.bfloat16)
    term = dot(hidden, down, NN)

    @pl.when(step == 0)
    def _():
        acc[...] = term

    @pl.when(step > 0)
    def _():
        acc[...] += term

    @pl.when(step == pl.num_programs(0) - 1)
    def _():
        out_ref[...] = acc[...].astype(out_ref.dtype)


def mlp(pieces, weights, out_type):
    shards, _, units, width = weights.shape
    many = 32
    count = sum(piece.shape[0] for piece in pieces)
    return pl.pallas_call(
        mlp_kernel,
        out_shape=jax.ShapeDtypeStruct((count, width), out_type),
        grid=(shards // many,),
        in_specs=[
            *[pl.BlockSpec(piece.shape, lambda i: (0, 0)) for piece in pieces],
            pl.BlockSpec((many, 1, units, width), lambda i: (i, 0, 0, 0)),
            pl.BlockSpec((many, 1, units, width), lambda i: (i, 1, 0, 0)),
        ],
        out_specs=pl.BlockSpec((count, width), lambda i: (0, 0)),
        scratch_shapes=[pltpu.VMEM((count, width), jnp.bfloat16), pltpu.VMEM((count, width), jnp.float32)],
        compiler_params=pltpu.CompilerParams(vmem_limit_bytes=56 << 20),
        cost_estimate=pl.CostEstimate(
            flops=4 * count * shards * units * width,
            bytes_accessed=4 * shards * units * width,
            transcendentals=0,
        ),
        name="mlp",
    )(*pieces, weights, weights)


def finish_kernel(mod_ref, w_ref, own_ref, back_ref, *refs):
    *resid, mine_ref, others_ref = refs
    prompts, half, rows = mine_ref.shape
    for p in range(prompts):
        span = slice(p * rows, (p + 1) * rows)
        total = own_ref[span, :] + back_ref[span, :].astype(jnp.float32)
        two = resid[p][...].astype(jnp.float32) + mod_ref[p, 5:6, :] * total
        last = layer_norm(two) * (1.0 + mod_ref[p, 9:10, :]) + mod_ref[p, 8:9, :]
        vel = dot(w_ref[...], last.astype(jnp.bfloat16), (((0,), (1,)), ((), ())))
        mine_ref[p] = vel[0:half]
        others_ref[p] = vel[half:].astype(jnp.bfloat16)


def finish(resid, own, back, mod, w_last):
    prompts = mod.shape[0]
    half = w_last.shape[1] // 2
    shape = (prompts, half, resid[0].shape[0])
    return pl.pallas_call(
        finish_kernel,
        out_shape=[jax.ShapeDtypeStruct(shape, jnp.float32), jax.ShapeDtypeStruct(shape, jnp.bfloat16)],
        compiler_params=pltpu.CompilerParams(vmem_limit_bytes=32 << 20),
        name="finish",
    )(mod, w_last, own, back, *resid)


def shifted(value, axis, by):
    size = lax.axis_size(axis)
    return lax.ppermute(value, axis, [(i, (i + by) % size) for i in range(size)])


def swap(value, axis):
    return shifted(value, axis, 1)


def local(
    img_state,
    txt_state,
    cond_vec,
    text_len,
    latent,
    w_mod,
    w_qkv_img,
    w_qkv_txt,
    w_attn_out,
    w_up,
    w_down,
    w_final,
):
    prompts = img_state.shape[1]
    rows = img_state.shape[2]
    width = img_state.shape[3]
    txt_rows = txt_state.shape[2]
    high = lax.axis_size("y")
    seqs = high * lax.axis_size("core")
    reqs = lax.axis_size("zhi") * lax.axis_size("x")
    everyone = reqs * seqs

    padding = jnp.zeros((prompts, TXT_PAD - txt_rows, width), jnp.bfloat16)
    mine = jnp.concatenate([img_state[0], txt_state[0], padding], axis=1)
    below, above = shifted(mine, "y", 1), shifted(mine, "y", -1)
    far = [shifted(below[p], "y", 1) if p % 2 == 0 else shifted(above[p], "y", -1) for p in range(prompts)]
    pairs = [mine, below, above]
    mates = [swap(block, "core") for block in pairs]
    tokens = [pairs + [far[p]] + mates + [swap(far[p], "core")] for p in range(prompts)]

    weights = lax.all_gather(jnp.stack([w_up, w_down])[None], REQ + SEQ, axis=0, tiled=True)

    cond_act = jax.nn.silu(cond_vec[0]).astype(jnp.bfloat16)
    part = dot(cond_act, w_mod, NT)
    cols = part.shape[1]
    lanes = -(-cols // 128) * 128
    part = jnp.pad(part, ((0, 0), (0, lanes - cols)))
    part = part.reshape(reqs, 1, prompts * lanes // 128, 128)
    part = jnp.broadcast_to(part, (reqs, seqs) + part.shape[2:]).reshape((everyone,) + part.shape[2:])
    got = lax.all_to_all(part, REQ + SEQ, 0, 0, tiled=True)
    got = got.reshape(everyone, prompts, lanes)[:, :, :cols]
    mod = jnp.swapaxes(got, 0, 1).reshape(prompts, 10, width)

    here, core = lax.axis_index("y"), lax.axis_index("core")
    level = (here + jnp.array([0, high - 1, 1, 2], jnp.int32)) % high
    owners = jnp.concatenate([2 * level + core, 2 * level + 1 - core]).astype(jnp.int32)
    inside = jnp.arange(TXT_PAD)
    index = owners[:, None] * txt_rows + inside[None, :]
    live = (inside < txt_rows)[None, None, :] & (index[None] < text_len[0][:, None, None])
    bias = jnp.where(live, 0.0, -1e30).astype(jnp.float32).reshape(prompts, seqs * TXT_PAD, 1)

    att = [
        attention(p, owners, tokens[p], mod, bias, w_qkv_img, w_qkv_txt) for p in range(prompts)
    ]
    late, _ = lax.optimization_barrier((w_attn_out, far[-1]))
    below, above = shifted(late, "y", 1), shifted(late, "y", -1)
    below, above, lead = lax.optimization_barrier((below, above, att[1]))
    cut = late.shape[0] // 2
    far = [shifted(below[:cut], "y", 1), shifted(above[cut:], "y", -1)]
    lead = lax.all_to_all(lead, SEQ, 0, 0, tiled=True)
    lead, far, below, above, last = lax.optimization_barrier((lead, far, below, above, att[0]))
    parts = [late, below, above] + list(far)
    parts = parts + [swap(part, "core") for part in parts]
    last = lax.all_to_all(last, SEQ, 0, 0, tiled=True)
    resid1, normed1 = project(1, owners, lead, parts, img_state, mod)
    other1 = swap(normed1, "cfg")
    resid0, normed0 = project(0, owners, pass_on(last), parts, img_state, mod)
    other0 = swap(normed0, "cfg")
    back = swap(mlp([other0, pass_on(other1)], weights, jnp.bfloat16), "cfg")
    own = mlp([normed0, normed1], weights, jnp.float32)
    resid = [resid0, resid1]

    half = latent.shape[2]
    branch = lax.axis_index("cfg")
    first = branch == 0
    w_last = jnp.where(first, w_final, jnp.concatenate([w_final[:, half:], w_final[:, :half]], axis=1))
    mine, others = finish(resid, own, back, mod, w_last)
    partner = swap(others, "cfg").astype(jnp.float32)
    cond_vel = jnp.where(first, mine, partner)
    uncond_vel = jnp.where(first, partner, mine)
    velocity = uncond_vel + 4.5 * (cond_vel - uncond_vel)
    latent_next = jnp.swapaxes(latent, 1, 2) - 0.04 * velocity
    return jnp.swapaxes(velocity, 1, 2), jnp.swapaxes(latent_next, 1, 2)


def solution(mesh):
    fine = Mesh(np.asarray(mesh.devices).reshape(2, 2, 4, 4, 2), ("cfg", "zhi", "x", "y", "core"))
    every = ("cfg",) + REQ + SEQ
    placed = (
        P("cfg", REQ, SEQ, None),
        P("cfg", REQ, SEQ, None),
        P("cfg", None, None),
        P("cfg", REQ),
        P(REQ, SEQ, "cfg"),
        P(REQ + SEQ, None),
        P(None, SEQ, None),
        P(None, SEQ, None),
        P(SEQ, None),
        P(every, None),
        P(every, None),
        P(),
    )
    return jax.shard_map(
        local,
        mesh=fine,
        in_specs=placed,
        out_specs=(P(REQ, SEQ, "cfg"), P(REQ, SEQ, "cfg")),
        check_vma=False,
    )
```

```python
import functools
import math

import jax
import jax.numpy as jnp
import numpy as np
from jax import lax
from jax.experimental import pallas as pl
from jax.experimental.pallas import tpu as pltpu
from jax.sharding import Mesh
from jax.sharding import PartitionSpec as P

HEAD = 64
SEQ = ("y", "core")
REQ = ("zhi", "x")
NT = (((1,), (1,)), ((), ()))
NN = (((1,), (0,)), ((), ()))
TN = (((0,), (0,)), ((), ()))
TXT_PAD = 32


def dot(a, b, dims):
    return lax.dot_general(a, b, dims, preferred_element_type=jnp.float32)


def layer_norm(value):
    mean = jnp.mean(value, axis=-1, keepdims=True)
    centered = value - mean
    spread = jnp.mean(centered * centered, axis=-1, keepdims=True)
    return centered * lax.rsqrt(spread + 1e-06)


def attn_kernel(prompt, many, idx_ref, *refs):
    pieces = refs[:many]
    mod_ref, bias_ref, wi_ref, wt_ref, out_ref, x_s, wi_s, wt_s, ai, at, k_s, v_s, q_s, x_sem, w_sem = refs[many:]
    block = x_s.shape[1]
    rows = block - TXT_PAD
    img = many * rows
    keys = many * block
    width = wt_s.shape[0] // 2
    heads = width // HEAD

    def take(s):
        piece = pieces[s] if len(pieces[s].shape) == 2 else pieces[s].at[prompt]
        return pltpu.make_async_copy(piece, x_s.at[s], x_sem.at[s])

    order = [(wi_ref, 0, wi_s, 0), (wi_ref, 2, wi_s, 1), (wi_ref, 1, wi_s, 2), (wt_ref, 2, wt_s, 0), (wt_ref, 1, wt_s, 1)]
    loads = [take(s) for s in range(many)] + [
        pltpu.make_async_copy(src.at[j], dst.at[pl.ds(i * width, width)], w_sem.at[n])
        for n, (src, j, dst, i) in enumerate(order)
    ]
    ahead = 3
    for load in loads[:ahead]:
        load.start()

    def modulated(part, scale, shift):
        normed = layer_norm(part.astype(jnp.float32))
        return (normed * (1.0 + mod_ref[0, scale : scale + 1, :]) + mod_ref[0, shift : shift + 1, :]).astype(
            jnp.bfloat16
        )

    def one_piece(s, carry):
        for n in range(many):

            @pl.when(s == n)
            def _(n=n):
                loads[n].wait()
                loads[n + ahead].start()

        ai[pl.ds(pl.multiple_of(s * rows, rows), rows), :] = modulated(x_s[s, 0:rows, :], 1, 0)
        at[pl.ds(pl.multiple_of(s * TXT_PAD, TXT_PAD), TXT_PAD), :] = modulated(x_s[s, rows:block, :], 7, 6)
        return carry

    lax.fori_loop(0, many, one_piece, 0)
    for load in loads[many + ahead :]:
        load.start()
    for load in loads[many:]:
        load.wait()
    ones = jnp.ones((16, keys), jnp.bfloat16)
    for h in range(heads):
        v_s[h, HEAD : HEAD + 16, :] = ones
        if h:
            q_s[h, 0 : h * HEAD, :] = jnp.zeros((h * HEAD, img), jnp.bfloat16)
        if h + 1 < heads:
            q_s[h, (h + 1) * HEAD :, :] = jnp.zeros((width - (h + 1) * HEAD, img), jnp.bfloat16)
    wide = 4 * rows

    def some_rows(c, carry):
        span = pl.ds(pl.multiple_of(c * wide, wide), wide)
        a = ai[span, :]
        k_s[span, :] = dot(a, wi_s[2 * width : 3 * width, :], NT).astype(jnp.bfloat16)
        both = dot(wi_s[0 : 2 * width, :], a, NT)
        query = (both[0:width] * (HEAD ** (-0.5) * math.log2(math.e))).astype(jnp.bfloat16)
        for h in range(heads):
            q_s[h, h * HEAD : (h + 1) * HEAD, span] = query[h * HEAD : (h + 1) * HEAD]
            v_s[h, 0:HEAD, span] = both[width + h * HEAD : width + (h + 1) * HEAD].astype(jnp.bfloat16)
        return carry

    lax.fori_loop(0, img // wide, some_rows, 0)
    a_txt = at[...]
    k_s[img:keys, :] = dot(a_txt, wt_s[width : 2 * width, :], NT).astype(jnp.bfloat16)
    v_txt = dot(wt_s[0:width, :], a_txt, NT).astype(jnp.bfloat16)
    for h in range(heads):
        v_s[h, 0:HEAD, img:keys] = v_txt[h * HEAD : (h + 1) * HEAD, :]

    def one_head(h, carry):
        query = q_s[h]
        s_img = dot(k_s[0:img, :], query, NN)
        s_txt = dot(k_s[img:keys, :], query, NN) + bias_ref[0]
        top = jnp.maximum(jnp.max(s_img, axis=0, keepdims=True), jnp.max(s_txt, axis=0, keepdims=True))
        p_img = jnp.exp2(s_img - top).astype(jnp.bfloat16)
        p_txt = jnp.exp2(s_txt - top).astype(jnp.bfloat16)
        o = dot(v_s[h, :, 0:img], p_img, NN) + dot(v_s[h, :, img:keys], p_txt, NN)
        o = (o[0:HEAD] / o[HEAD : HEAD + 1]).astype(jnp.bfloat16)
        for i in range(many):
            out_ref[idx_ref[i], pl.ds(pl.multiple_of(h * HEAD, HEAD), HEAD), :] = o[:, i * rows : (i + 1) * rows]
        return carry

    lax.fori_loop(0, heads, one_head, 0)


def attention(prompt, owners, pieces, mod, bias, w_img, w_txt):
    many = len(pieces)
    block, depth = pieces[0].shape[-2:]
    rows = block - TXT_PAD
    width = w_img.shape[1]
    heads = width // HEAD
    keys = many * block
    once = lambda *zeros: (lambda i, owners: zeros)
    stays = pl.BlockSpec(memory_space=pltpu.HBM)
    bf16 = jnp.bfloat16
    return pl.pallas_call(
        functools.partial(attn_kernel, prompt, many),
        out_shape=jax.ShapeDtypeStruct((many, width, rows), bf16),
        grid_spec=pltpu.PrefetchScalarGridSpec(
            num_scalar_prefetch=1,
            grid=(1,),
            in_specs=[stays] * many
            + [
                pl.BlockSpec((1, 10, depth), once(prompt, 0, 0)),
                pl.BlockSpec((1, many * TXT_PAD, 1), once(prompt, 0, 0)),
                stays,
                stays,
            ],
            out_specs=pl.BlockSpec((many, width, rows), once(0, 0, 0)),
            scratch_shapes=[
                pltpu.VMEM((many, block, depth), bf16),
                pltpu.VMEM((3 * width, depth), bf16),
                pltpu.VMEM((2 * width, depth), bf16),
                pltpu.VMEM((many * rows, depth), bf16),
                pltpu.VMEM((many * TXT_PAD, depth), bf16),
                pltpu.VMEM((keys, width), bf16),
                pltpu.VMEM((heads, HEAD + 16, keys), bf16),
                pltpu.VMEM((heads, width, many * rows), bf16),
                pltpu.SemaphoreType.DMA((many,)),
                pltpu.SemaphoreType.DMA((5,)),
            ],
        ),
        compiler_params=pltpu.CompilerParams(vmem_limit_bytes=56 << 20),
        cost_estimate=pl.CostEstimate(flops=8000000000, bytes_accessed=8000000, transcendentals=0),
        name="attn",
    )(owners, *pieces, mod, bias, w_img, w_txt)


def pass_on(value):
    anywhere = pl.BlockSpec(memory_space=pl.ANY)
    return pl.pallas_call(
        lambda value_ref, out_ref: None,
        out_shape=jax.ShapeDtypeStruct(value.shape, value.dtype),
        in_specs=[anywhere],
        out_specs=anywhere,
        input_output_aliases={0: 0},
        cost_estimate=pl.CostEstimate(flops=4000000000, bytes_accessed=8000000, transcendentals=0),
        name="pass_on",
    )(value)


def proj_kernel(many, idx_ref, att_ref, *refs):
    parts = refs[:many]
    img_ref, mod_ref, resid_ref, normed_ref, w_s, att_s, sem = refs[many:]
    size = att_ref.shape[1]
    loads, at = [], 0
    for n, part in enumerate(parts):
        loads.append(pltpu.make_async_copy(part, w_s.at[pl.ds(at, part.shape[0])], sem.at[n]))
        at += part.shape[0]
    for load in loads:
        load.start()
    for s in range(att_ref.shape[0]):
        att_s[s * size : (s + 1) * size, :] = att_ref[idx_ref[s]]
    for load in loads:
        load.wait()
    total = dot(att_s[...], w_s[...], TN)
    one = (img_ref[0, 0].astype(jnp.float32) + mod_ref[0, 2:3, :] * total).astype(jnp.bfloat16)
    resid_ref[...] = one
    normed = layer_norm(one.astype(jnp.float32)) * (1.0 + mod_ref[0, 4:5, :]) + mod_ref[0, 3:4, :]
    normed_ref[...] = normed.astype(jnp.bfloat16)


def project(prompt, owners, att, parts, img_state, mod):
    rows, depth = img_state.shape[2:]
    many = len(parts)
    total = att.shape[0] * att.shape[1]
    once = lambda *zeros: (lambda i, owners: zeros)
    return pl.pallas_call(
        functools.partial(proj_kernel, many),
        out_shape=[jax.ShapeDtypeStruct((rows, depth), jnp.bfloat16)] * 2,
        grid_spec=pltpu.PrefetchScalarGridSpec(
            num_scalar_prefetch=1,
            grid=(1,),
            in_specs=[pl.BlockSpec(att.shape, once(0, 0, 0))]
            + [pl.BlockSpec(memory_space=pltpu.HBM)] * many
            + [
                pl.BlockSpec((1, 1, rows, depth), once(0, prompt, 0, 0)),
                pl.BlockSpec((1, 10, depth), once(prompt, 0, 0)),
            ],
            out_specs=[pl.BlockSpec((rows, depth), once(0, 0))] * 2,
            scratch_shapes=[
                pltpu.VMEM((total, depth), jnp.bfloat16),
                pltpu.VMEM((total, rows), jnp.bfloat16),
                pltpu.SemaphoreType.DMA((many,)),
            ],
        ),
        compiler_params=pltpu.CompilerParams(vmem_limit_bytes=56 << 20),
        cost_estimate=pl.CostEstimate(flops=8000000000, bytes_accessed=5000000, transcendentals=0),
        name="proj",
    )(owners, att, *parts, img_state, mod)


def mlp_kernel(*refs):
    *pieces, up_ref, down_ref, out_ref, x_s, acc = refs
    step = pl.program_id(0)

    @pl.when(step == 0)
    def _():
        at = 0
        for piece in pieces:
            x_s[at : at + piece.shape[0], :] = piece[...]
            at += piece.shape[0]

    depth = up_ref.shape[-1]
    up = up_ref[...].reshape(-1, depth)
    down = down_ref[...].reshape(-1, depth)
    hidden = jax.nn.gelu(dot(x_s[...], up, NT), approximate=True).astype(jnp.bfloat16)
    term = dot(hidden, down, NN)

    @pl.when(step == 0)
    def _():
        acc[...] = term

    @pl.when(step > 0)
    def _():
        acc[...] += term

    @pl.when(step == pl.num_programs(0) - 1)
    def _():
        out_ref[...] = acc[...].astype(out_ref.dtype)


def mlp(pieces, weights, out_type):
    shards, _, units, width = weights.shape
    many = 32
    count = sum(piece.shape[0] for piece in pieces)
    return pl.pallas_call(
        mlp_kernel,
        out_shape=jax.ShapeDtypeStruct((count, width), out_type),
        grid=(shards // many,),
        in_specs=[
            *[pl.BlockSpec(piece.shape, lambda i: (0, 0)) for piece in pieces],
            pl.BlockSpec((many, 1, units, width), lambda i: (i, 0, 0, 0)),
            pl.BlockSpec((many, 1, units, width), lambda i: (i, 1, 0, 0)),
        ],
        out_specs=pl.BlockSpec((count, width), lambda i: (0, 0)),
        scratch_shapes=[pltpu.VMEM((count, width), jnp.bfloat16), pltpu.VMEM((count, width), jnp.float32)],
        compiler_params=pltpu.CompilerParams(vmem_limit_bytes=56 << 20),
        cost_estimate=pl.CostEstimate(
            flops=4 * count * shards * units * width,
            bytes_accessed=4 * shards * units * width,
            transcendentals=0,
        ),
        name="mlp",
    )(*pieces, weights, weights)


def finish_kernel(mod_ref, w_ref, own_ref, back_ref, *refs):
    *resid, mine_ref, others_ref = refs
    prompts, half, rows = mine_ref.shape
    for p in range(prompts):
        span = slice(p * rows, (p + 1) * rows)
        total = own_ref[span, :] + back_ref[span, :].astype(jnp.float32)
        two = resid[p][...].astype(jnp.float32) + mod_ref[p, 5:6, :] * total
        last = layer_norm(two) * (1.0 + mod_ref[p, 9:10, :]) + mod_ref[p, 8:9, :]
        vel = dot(w_ref[...], last.astype(jnp.bfloat16), (((0,), (1,)), ((), ())))
        mine_ref[p] = vel[0:half]
        others_ref[p] = vel[half:].astype(jnp.bfloat16)


def finish(resid, own, back, mod, w_last):
    prompts = mod.shape[0]
    half = w_last.shape[1] // 2
    shape = (prompts, half, resid[0].shape[0])
    return pl.pallas_call(
        finish_kernel,
        out_shape=[jax.ShapeDtypeStruct(shape, jnp.float32), jax.ShapeDtypeStruct(shape, jnp.bfloat16)],
        compiler_params=pltpu.CompilerParams(vmem_limit_bytes=32 << 20),
        name="finish",
    )(mod, w_last, own, back, *resid)


def shifted(value, axis, by):
    size = lax.axis_size(axis)
    return lax.ppermute(value, axis, [(i, (i + by) % size) for i in range(size)])


def swap(value, axis):
    return shifted(value, axis, 1)


def local(
    img_state,
    txt_state,
    cond_vec,
    text_len,
    latent,
    w_mod,
    w_qkv_img,
    w_qkv_txt,
    w_attn_out,
    w_up,
    w_down,
    w_final,
):
    prompts = img_state.shape[1]
    rows = img_state.shape[2]
    width = img_state.shape[3]
    txt_rows = txt_state.shape[2]
    high = lax.axis_size("y")
    seqs = high * lax.axis_size("core")
    reqs = lax.axis_size("zhi") * lax.axis_size("x")
    everyone = reqs * seqs

    padding = jnp.zeros((prompts, TXT_PAD - txt_rows, width), jnp.bfloat16)
    mine = jnp.concatenate([img_state[0], txt_state[0], padding], axis=1)
    below, above = shifted(mine, "y", 1), shifted(mine, "y", -1)
    far = [shifted(below[p], "y", 1) if p % 2 == 0 else shifted(above[p], "y", -1) for p in range(prompts)]
    pairs = [mine, below, above]
    mates = [swap(block, "core") for block in pairs]
    tokens = [pairs + [far[p]] + mates + [swap(far[p], "core")] for p in range(prompts)]

    weights = lax.all_gather(jnp.stack([w_up, w_down])[None], REQ + SEQ, axis=0, tiled=True)

    cond_act = jax.nn.silu(cond_vec[0]).astype(jnp.bfloat16)
    part = dot(cond_act, w_mod, NT)
    cols = part.shape[1]
    lanes = -(-cols // 128) * 128
    part = jnp.pad(part, ((0, 0), (0, lanes - cols)))
    part = part.reshape(reqs, 1, prompts * lanes // 128, 128)
    part = jnp.broadcast_to(part, (reqs, seqs) + part.shape[2:]).reshape((everyone,) + part.shape[2:])
    got = lax.all_to_all(part, REQ + SEQ, 0, 0, tiled=True)
    got = got.reshape(everyone, prompts, lanes)[:, :, :cols]
    mod = jnp.swapaxes(got, 0, 1).reshape(prompts, 10, width)

    here, core = lax.axis_index("y"), lax.axis_index("core")
    level = (here + jnp.array([0, high - 1, 1, 2], jnp.int32)) % high
    owners = jnp.concatenate([2 * level + core, 2 * level + 1 - core]).astype(jnp.int32)
    inside = jnp.arange(TXT_PAD)
    index = owners[:, None] * txt_rows + inside[None, :]
    live = (inside < txt_rows)[None, None, :] & (index[None] < text_len[0][:, None, None])
    bias = jnp.where(live, 0.0, -1e30).astype(jnp.float32).reshape(prompts, seqs * TXT_PAD, 1)

    att = [
        attention(p, owners, tokens[p], mod, bias, w_qkv_img, w_qkv_txt) for p in range(prompts)
    ]
    late, _ = lax.optimization_barrier((w_attn_out, far[-1]))
    below, above = shifted(late, "y", 1), shifted(late, "y", -1)
    below, above, lead = lax.optimization_barrier((below, above, att[1]))
    cut = late.shape[0] // 2
    far = [shifted(below[:cut], "y", 1), shifted(above[cut:], "y", -1)]
    lead = lax.all_to_all(lead, SEQ, 0, 0, tiled=True)
    lead, far, below, above, last = lax.optimization_barrier((lead, far, below, above, att[0]))
    parts = [late, below, above] + list(far)
    parts = parts + [swap(part, "core") for part in parts]
    last = lax.all_to_all(last, SEQ, 0, 0, tiled=True)
    resid1, normed1 = project(1, owners, lead, parts, img_state, mod)
    other1 = swap(normed1, "cfg")
    resid0, normed0 = project(0, owners, pass_on(last), parts, img_state, mod)
    other0 = swap(normed0, "cfg")
    back = swap(mlp([other0, pass_on(other1)], weights, jnp.bfloat16), "cfg")
    own = mlp([normed0, normed1], weights, jnp.float32)
    resid = [resid0, resid1]

    half = latent.shape[2]
    branch = lax.axis_index("cfg")
    first = branch == 0
    w_last = jnp.where(first, w_final, jnp.concatenate([w_final[:, half:], w_final[:, :half]], axis=1))
    mine, others = finish(resid, own, back, mod, w_last)
    partner = swap(others, "cfg").astype(jnp.float32)
    cond_vel = jnp.where(first, mine, partner)
    uncond_vel = jnp.where(first, partner, mine)
    velocity = uncond_vel + 4.5 * (cond_vel - uncond_vel)
    latent_next = jnp.swapaxes(latent, 1, 2) - 0.04 * velocity
    return jnp.swapaxes(velocity, 1, 2), jnp.swapaxes(latent_next, 1, 2)


def solution(mesh):
    fine = Mesh(np.asarray(mesh.devices).reshape(2, 2, 4, 4, 2), ("cfg", "zhi", "x", "y", "core"))
    every = ("cfg",) + REQ + SEQ
    placed = (
        P("cfg", REQ, SEQ, None),
        P("cfg", REQ, SEQ, None),
        P("cfg", None, None),
        P("cfg", REQ),
        P(REQ, SEQ, "cfg"),
        P(REQ + SEQ, None),
        P(None, SEQ, None),
        P(None, SEQ, None),
        P(SEQ, None),
        P(every, None),
        P(every, None),
        P(),
    )
    return jax.shard_map(
        local,
        mesh=fine,
        in_specs=placed,
        out_specs=(P(REQ, SEQ, "cfg"), P(REQ, SEQ, "cfg")),
        check_vma=False,
    )
```

```python
import functools
import math

import jax
import jax.numpy as jnp
import numpy as np
from jax import lax
from jax.experimental import pallas as pl
from jax.experimental.pallas import tpu as pltpu
from jax.sharding import Mesh
from jax.sharding import PartitionSpec as P

HEAD = 64
SEQ = ("y", "core")
REQ = ("zhi", "x")
NT = (((1,), (1,)), ((), ()))
NN = (((1,), (0,)), ((), ()))
TN = (((0,), (0,)), ((), ()))
TXT_PAD = 32


def dot(a, b, dims):
    return lax.dot_general(a, b, dims, preferred_element_type=jnp.float32)


def layer_norm(value):
    mean = jnp.mean(value, axis=-1, keepdims=True)
    centered = value - mean
    spread = jnp.mean(centered * centered, axis=-1, keepdims=True)
    return centered * lax.rsqrt(spread + 1e-06)


def attn_kernel(prompt, many, idx_ref, *refs):
    pieces = refs[:many]
    mod_ref, bias_ref, wi_ref, wt_ref, out_ref, x_s, wi_s, wt_s, ai, at, k_s, v_s, q_s, x_sem, w_sem = refs[many:]
    block = x_s.shape[1]
    rows = block - TXT_PAD
    img = many * rows
    keys = many * block
    width = wt_s.shape[0] // 2
    heads = width // HEAD

    def take(s):
        piece = pieces[s] if len(pieces[s].shape) == 2 else pieces[s].at[prompt]
        return pltpu.make_async_copy(piece, x_s.at[s], x_sem.at[s])

    order = [(wi_ref, 0, wi_s, 0), (wi_ref, 2, wi_s, 1), (wi_ref, 1, wi_s, 2), (wt_ref, 2, wt_s, 0), (wt_ref, 1, wt_s, 1)]
    loads = [take(s) for s in range(many)] + [
        pltpu.make_async_copy(src.at[j], dst.at[pl.ds(i * width, width)], w_sem.at[n])
        for n, (src, j, dst, i) in enumerate(order)
    ]
    ahead = 3
    for load in loads[:ahead]:
        load.start()

    def modulated(part, scale, shift):
        normed = layer_norm(part.astype(jnp.float32))
        return (normed * (1.0 + mod_ref[0, scale : scale + 1, :]) + mod_ref[0, shift : shift + 1, :]).astype(
            jnp.bfloat16
        )

    def one_piece(s, carry):
        for n in range(many):

            @pl.when(s == n)
            def _(n=n):
                loads[n].wait()
                loads[n + ahead].start()

        ai[pl.ds(pl.multiple_of(s * rows, rows), rows), :] = modulated(x_s[s, 0:rows, :], 1, 0)
        at[pl.ds(pl.multiple_of(s * TXT_PAD, TXT_PAD), TXT_PAD), :] = modulated(x_s[s, rows:block, :], 7, 6)
        return carry

    lax.fori_loop(0, many, one_piece, 0)
    for load in loads[many + ahead :]:
        load.start()
    for load in loads[many:]:
        load.wait()
    ones = jnp.ones((16, keys), jnp.bfloat16)
    for h in range(heads):
        v_s[h, HEAD : HEAD + 16, :] = ones
        if h:
            q_s[h, 0 : h * HEAD, :] = jnp.zeros((h * HEAD, img), jnp.bfloat16)
        if h + 1 < heads:
            q_s[h, (h + 1) * HEAD :, :] = jnp.zeros((width - (h + 1) * HEAD, img), jnp.bfloat16)
    wide = 4 * rows

    def some_rows(c, carry):
        span = pl.ds(pl.multiple_of(c * wide, wide), wide)
        a = ai[span, :]
        k_s[span, :] = dot(a, wi_s[2 * width : 3 * width, :], NT).astype(jnp.bfloat16)
        both = dot(wi_s[0 : 2 * width, :], a, NT)
        query = (both[0:width] * (HEAD ** (-0.5) * math.log2(math.e))).astype(jnp.bfloat16)
        for h in range(heads):
            q_s[h, h * HEAD : (h + 1) * HEAD, span] = query[h * HEAD : (h + 1) * HEAD]
            v_s[h, 0:HEAD, span] = both[width + h * HEAD : width + (h + 1) * HEAD].astype(jnp.bfloat16)
        return carry

    lax.fori_loop(0, img // wide, some_rows, 0)
    a_txt = at[...]
    k_s[img:keys, :] = dot(a_txt, wt_s[width : 2 * width, :], NT).astype(jnp.bfloat16)
    v_txt = dot(wt_s[0:width, :], a_txt, NT).astype(jnp.bfloat16)
    for h in range(heads):
        v_s[h, 0:HEAD, img:keys] = v_txt[h * HEAD : (h + 1) * HEAD, :]

    def one_head(h, carry):
        query = q_s[h]
        s_img = dot(k_s[0:img, :], query, NN)
        s_txt = dot(k_s[img:keys, :], query, NN) + bias_ref[0]
        top = jnp.maximum(jnp.max(s_img, axis=0, keepdims=True), jnp.max(s_txt, axis=0, keepdims=True))
        p_img = jnp.exp2(s_img - top).astype(jnp.bfloat16)
        p_txt = jnp.exp2(s_txt - top).astype(jnp.bfloat16)
        o = dot(v_s[h, :, 0:img], p_img, NN) + dot(v_s[h, :, img:keys], p_txt, NN)
        o = (o[0:HEAD] / o[HEAD : HEAD + 1]).astype(jnp.bfloat16)
        for i in range(many):
            out_ref[idx_ref[i], pl.ds(pl.multiple_of(h * HEAD, HEAD), HEAD), :] = o[:, i * rows : (i + 1) * rows]
        return carry

    lax.fori_loop(0, heads, one_head, 0)


def attention(prompt, owners, pieces, mod, bias, w_img, w_txt):
    many = len(pieces)
    block, depth = pieces[0].shape[-2:]
    rows = block - TXT_PAD
    width = w_img.shape[1]
    heads = width // HEAD
    keys = many * block
    once = lambda *zeros: (lambda i, owners: zeros)
    stays = pl.BlockSpec(memory_space=pltpu.HBM)
    bf16 = jnp.bfloat16
    return pl.pallas_call(
        functools.partial(attn_kernel, prompt, many),
        out_shape=jax.ShapeDtypeStruct((many, width, rows), bf16),
        grid_spec=pltpu.PrefetchScalarGridSpec(
            num_scalar_prefetch=1,
            grid=(1,),
            in_specs=[stays] * many
            + [
                pl.BlockSpec((1, 10, depth), once(prompt, 0, 0)),
                pl.BlockSpec((1, many * TXT_PAD, 1), once(prompt, 0, 0)),
                stays,
                stays,
            ],
            out_specs=pl.BlockSpec((many, width, rows), once(0, 0, 0)),
            scratch_shapes=[
                pltpu.VMEM((many, block, depth), bf16),
                pltpu.VMEM((3 * width, depth), bf16),
                pltpu.VMEM((2 * width, depth), bf16),
                pltpu.VMEM((many * rows, depth), bf16),
                pltpu.VMEM((many * TXT_PAD, depth), bf16),
                pltpu.VMEM((keys, width), bf16),
                pltpu.VMEM((heads, HEAD + 16, keys), bf16),
                pltpu.VMEM((heads, width, many * rows), bf16),
                pltpu.SemaphoreType.DMA((many,)),
                pltpu.SemaphoreType.DMA((5,)),
            ],
        ),
        compiler_params=pltpu.CompilerParams(vmem_limit_bytes=56 << 20),
        cost_estimate=pl.CostEstimate(flops=8000000000, bytes_accessed=8000000, transcendentals=0),
        name="attn",
    )(owners, *pieces, mod, bias, w_img, w_txt)


def pass_on(value):
    anywhere = pl.BlockSpec(memory_space=pl.ANY)
    return pl.pallas_call(
        lambda value_ref, out_ref: None,
        out_shape=jax.ShapeDtypeStruct(value.shape, value.dtype),
        in_specs=[anywhere],
        out_specs=anywhere,
        input_output_aliases={0: 0},
        cost_estimate=pl.CostEstimate(flops=4000000000, bytes_accessed=8000000, transcendentals=0),
        name="pass_on",
    )(value)


def proj_kernel(many, idx_ref, att_ref, *refs):
    parts = refs[:many]
    img_ref, mod_ref, resid_ref, normed_ref, w_s, att_s, sem = refs[many:]
    size = att_ref.shape[1]
    loads, at = [], 0
    for n, part in enumerate(parts):
        loads.append(pltpu.make_async_copy(part, w_s.at[pl.ds(at, part.shape[0])], sem.at[n]))
        at += part.shape[0]
    for load in loads:
        load.start()
    for s in range(att_ref.shape[0]):
        att_s[s * size : (s + 1) * size, :] = att_ref[idx_ref[s]]
    for load in loads:
        load.wait()
    total = dot(att_s[...], w_s[...], TN)
    one = (img_ref[0, 0].astype(jnp.float32) + mod_ref[0, 2:3, :] * total).astype(jnp.bfloat16)
    resid_ref[...] = one
    normed = layer_norm(one.astype(jnp.float32)) * (1.0 + mod_ref[0, 4:5, :]) + mod_ref[0, 3:4, :]
    normed_ref[...] = normed.astype(jnp.bfloat16)


def project(prompt, owners, att, parts, img_state, mod):
    rows, depth = img_state.shape[2:]
    many = len(parts)
    total = att.shape[0] * att.shape[1]
    once = lambda *zeros: (lambda i, owners: zeros)
    return pl.pallas_call(
        functools.partial(proj_kernel, many),
        out_shape=[jax.ShapeDtypeStruct((rows, depth), jnp.bfloat16)] * 2,
        grid_spec=pltpu.PrefetchScalarGridSpec(
            num_scalar_prefetch=1,
            grid=(1,),
            in_specs=[pl.BlockSpec(att.shape, once(0, 0, 0))]
            + [pl.BlockSpec(memory_space=pltpu.HBM)] * many
            + [
                pl.BlockSpec((1, 1, rows, depth), once(0, prompt, 0, 0)),
                pl.BlockSpec((1, 10, depth), once(prompt, 0, 0)),
            ],
            out_specs=[pl.BlockSpec((rows, depth), once(0, 0))] * 2,
            scratch_shapes=[
                pltpu.VMEM((total, depth), jnp.bfloat16),
                pltpu.VMEM((total, rows), jnp.bfloat16),
                pltpu.SemaphoreType.DMA((many,)),
            ],
        ),
        compiler_params=pltpu.CompilerParams(vmem_limit_bytes=56 << 20),
        cost_estimate=pl.CostEstimate(flops=8000000000, bytes_accessed=5000000, transcendentals=0),
        name="proj",
    )(owners, att, *parts, img_state, mod)


def mlp_kernel(*refs):
    *pieces, up_ref, down_ref, out_ref, x_s, acc = refs
    step = pl.program_id(0)

    @pl.when(step == 0)
    def _():
        at = 0
        for piece in pieces:
            x_s[at : at + piece.shape[0], :] = piece[...]
            at += piece.shape[0]

    depth = up_ref.shape[-1]
    up = up_ref[...].reshape(-1, depth)
    down = down_ref[...].reshape(-1, depth)
    hidden = jax.nn.gelu(dot(x_s[...], up, NT), approximate=True).astype(jnp.bfloat16)
    term = dot(hidden, down, NN)

    @pl.when(step == 0)
    def _():
        acc[...] = term

    @pl.when(step > 0)
    def _():
        acc[...] += term

    @pl.when(step == pl.num_programs(0) - 1)
    def _():
        out_ref[...] = acc[...].astype(out_ref.dtype)


def mlp(pieces, weights, out_type):
    shards, _, units, width = weights.shape
    many = 32
    count = sum(piece.shape[0] for piece in pieces)
    return pl.pallas_call(
        mlp_kernel,
        out_shape=jax.ShapeDtypeStruct((count, width), out_type),
        grid=(shards // many,),
        in_specs=[
            *[pl.BlockSpec(piece.shape, lambda i: (0, 0)) for piece in pieces],
            pl.BlockSpec((many, 1, units, width), lambda i: (i, 0, 0, 0)),
            pl.BlockSpec((many, 1, units, width), lambda i: (i, 1, 0, 0)),
        ],
        out_specs=pl.BlockSpec((count, width), lambda i: (0, 0)),
        scratch_shapes=[pltpu.VMEM((count, width), jnp.bfloat16), pltpu.VMEM((count, width), jnp.float32)],
        compiler_params=pltpu.CompilerParams(vmem_limit_bytes=56 << 20),
        cost_estimate=pl.CostEstimate(
            flops=4 * count * shards * units * width,
            bytes_accessed=4 * shards * units * width,
            transcendentals=0,
        ),
        name="mlp",
    )(*pieces, weights, weights)


def finish_kernel(mod_ref, w_ref, own_ref, back_ref, *refs):
    *resid, mine_ref, others_ref = refs
    prompts, half, rows = mine_ref.shape
    for p in range(prompts):
        span = slice(p * rows, (p + 1) * rows)
        total = own_ref[span, :] + back_ref[span, :].astype(jnp.float32)
        two = resid[p][...].astype(jnp.float32) + mod_ref[p, 5:6, :] * total
        last = layer_norm(two) * (1.0 + mod_ref[p, 9:10, :]) + mod_ref[p, 8:9, :]
        vel = dot(w_ref[...], last.astype(jnp.bfloat16), (((0,), (1,)), ((), ())))
        mine_ref[p] = vel[0:half]
        others_ref[p] = vel[half:].astype(jnp.bfloat16)


def finish(resid, own, back, mod, w_last):
    prompts = mod.shape[0]
    half = w_last.shape[1] // 2
    shape = (prompts, half, resid[0].shape[0])
    return pl.pallas_call(
        finish_kernel,
        out_shape=[jax.ShapeDtypeStruct(shape, jnp.float32), jax.ShapeDtypeStruct(shape, jnp.bfloat16)],
        compiler_params=pltpu.CompilerParams(vmem_limit_bytes=32 << 20),
        name="finish",
    )(mod, w_last, own, back, *resid)


def shifted(value, axis, by):
    size = lax.axis_size(axis)
    return lax.ppermute(value, axis, [(i, (i + by) % size) for i in range(size)])


def swap(value, axis):
    return shifted(value, axis, 1)


def local(
    img_state,
    txt_state,
    cond_vec,
    text_len,
    latent,
    w_mod,
    w_qkv_img,
    w_qkv_txt,
    w_attn_out,
    w_up,
    w_down,
    w_final,
):
    prompts = img_state.shape[1]
    rows = img_state.shape[2]
    width = img_state.shape[3]
    txt_rows = txt_state.shape[2]
    high = lax.axis_size("y")
    seqs = high * lax.axis_size("core")
    reqs = lax.axis_size("zhi") * lax.axis_size("x")
    everyone = reqs * seqs

    padding = jnp.zeros((prompts, TXT_PAD - txt_rows, width), jnp.bfloat16)
    mine = jnp.concatenate([img_state[0], txt_state[0], padding], axis=1)
    below, above = shifted(mine, "y", 1), shifted(mine, "y", -1)
    far = [shifted(below[p], "y", 1) if p % 2 == 0 else shifted(above[p], "y", -1) for p in range(prompts)]
    pairs = [mine, below, above]
    mates = [swap(block, "core") for block in pairs]
    tokens = [pairs + [far[p]] + mates + [swap(far[p], "core")] for p in range(prompts)]

    up, down, _ = lax.optimization_barrier((w_up, w_down, mine))
    weights = lax.all_gather(jnp.stack([up, down])[None], REQ + SEQ, axis=0, tiled=True)

    cond_act = jax.nn.silu(cond_vec[0]).astype(jnp.bfloat16)
    part = dot(cond_act, w_mod, NT)
    cols = part.shape[1]
    lanes = -(-cols // 128) * 128
    part = jnp.pad(part, ((0, 0), (0, lanes - cols)))
    part = part.reshape(reqs, 1, prompts * lanes // 128, 128)
    part = jnp.broadcast_to(part, (reqs, seqs) + part.shape[2:]).reshape((everyone,) + part.shape[2:])
    got = lax.all_to_all(part, REQ + SEQ, 0, 0, tiled=True)
    got = got.reshape(everyone, prompts, lanes)[:, :, :cols]
    mod = jnp.swapaxes(got, 0, 1).reshape(prompts, 10, width)

    here, core = lax.axis_index("y"), lax.axis_index("core")
    level = (here + jnp.array([0, high - 1, 1, 2], jnp.int32)) % high
    owners = jnp.concatenate([2 * level + core, 2 * level + 1 - core]).astype(jnp.int32)
    inside = jnp.arange(TXT_PAD)
    index = owners[:, None] * txt_rows + inside[None, :]
    live = (inside < txt_rows)[None, None, :] & (index[None] < text_len[0][:, None, None])
    bias = jnp.where(live, 0.0, -1e30).astype(jnp.float32).reshape(prompts, seqs * TXT_PAD, 1)

    att = [
        attention(p, owners, tokens[p], mod, bias, w_qkv_img, w_qkv_txt) for p in range(prompts)
    ]
    late, _ = lax.optimization_barrier((w_attn_out, far[-1]))
    below, above = shifted(late, "y", 1), shifted(late, "y", -1)
    below, above, lead = lax.optimization_barrier((below, above, att[1]))
    cut = late.shape[0] // 2
    far = [shifted(below[:cut], "y", 1), shifted(above[cut:], "y", -1)]
    lead = lax.all_to_all(lead, SEQ, 0, 0, tiled=True)
    lead, far, below, above, last = lax.optimization_barrier((lead, far, below, above, att[0]))
    parts = [late, below, above] + list(far)
    parts = parts + [swap(part, "core") for part in parts]
    last = lax.all_to_all(last, SEQ, 0, 0, tiled=True)
    resid1, normed1 = project(1, owners, lead, parts, img_state, mod)
    other1 = swap(normed1, "cfg")
    resid0, normed0 = project(0, owners, pass_on(last), parts, img_state, mod)
    other0 = swap(normed0, "cfg")
    back = swap(mlp([other0, pass_on(other1)], weights, jnp.bfloat16), "cfg")
    own = mlp([normed0, normed1], weights, jnp.float32)
    resid = [resid0, resid1]

    half = latent.shape[2]
    branch = lax.axis_index("cfg")
    first = branch == 0
    w_last = jnp.where(first, w_final, jnp.concatenate([w_final[:, half:], w_final[:, :half]], axis=1))
    mine, others = finish(resid, own, back, mod, w_last)
    partner = swap(others, "cfg").astype(jnp.float32)
    cond_vel = jnp.where(first, mine, partner)
    uncond_vel = jnp.where(first, partner, mine)
    velocity = uncond_vel + 4.5 * (cond_vel - uncond_vel)
    latent_next = jnp.swapaxes(latent, 1, 2) - 0.04 * velocity
    return jnp.swapaxes(velocity, 1, 2), jnp.swapaxes(latent_next, 1, 2)


def solution(mesh):
    fine = Mesh(np.asarray(mesh.devices).reshape(2, 2, 4, 4, 2), ("cfg", "zhi", "x", "y", "core"))
    every = ("cfg",) + REQ + SEQ
    placed = (
        P("cfg", REQ, SEQ, None),
        P("cfg", REQ, SEQ, None),
        P("cfg", None, None),
        P("cfg", REQ),
        P(REQ, SEQ, "cfg"),
        P(REQ + SEQ, None),
        P(None, SEQ, None),
        P(None, SEQ, None),
        P(SEQ, None),
        P(every, None),
        P(every, None),
        P(),
    )
    return jax.shard_map(
        local,
        mesh=fine,
        in_specs=placed,
        out_specs=(P(REQ, SEQ, "cfg"), P(REQ, SEQ, "cfg")),
        check_vma=False,
    )
```
